512 devices in a mesh: guide: 2 (over x_lo), seq: 32 (over x_hi, z), blk: 8 (over y, core).
Axes of the slice: x: 4 (x_hi: 2, x_lo: 2; x = x_hi * 2 + x_lo), y: 4, z: 16, core: 2. Of those that a mesh axis runs over, the one named last changes fastest.
Arguments:
- img_hidden: bfloat16 [2, 2, 2048, 3072], P('guide', None, 'seq', 'blk'), may hold values from -6 to 6
- img_query: bfloat16 [2, 2, 2048, 3072], P('guide', None, 'seq', 'blk')
- img_key: bfloat16 [2, 2, 2048, 3072], P('guide', None, 'seq', 'blk')
- img_value: bfloat16 [2, 2, 2048, 3072], P('guide', None, 'seq', 'blk'), may hold values from -6 to 6
- txt_key: bfloat16 [2, 2, 512, 3072], P('guide', None, 'seq', 'blk'), may hold values from -6 to 6
- txt_value: bfloat16 [2, 2, 512, 3072], P('guide', None, 'seq', 'blk'), may hold values from -6 to 6
- query_gain: float32 [128], replicated
- key_gain: float32 [2, 128], replicated
- gate: float32 [2, 2, 3072], P('guide', None, 'blk'), may hold values from -4 to 4
- proj_weight: bfloat16 [3072, 3072], P('blk'), may hold values from -0.15625 to 0.15625
- proj_bias: float32 [3072], P('blk'), may hold values from -3 to 3
- guidance: float32 [2], replicated, may hold values from 1.5 to 5
- text_len: int32 [2], replicated, may hold values from 1 to 512, as said below
- step_index: int32 [1], replicated, may hold values from 0 to 7
- latent: bfloat16 [2, 2048, 3072], P('guide', 'seq', 'blk'), may hold values from -6 to 6
Outputs:
- guided: bfloat16 [2, 2048, 3072], P('guide', 'seq', 'blk')
- next_state: bfloat16 [2, 2048, 3072], P('guide', 'seq', 'blk')
The draws below stay inside these ranges and needn't reach their ends.
Inputs may be any that keep to these rules, and one draw needn't show every extreme that they name: `text_len`: some prompt has all 512 text slots live.
All inputs are finite; a program needn't handle non-finite values.
Results may differ from the reference program's by a relative error of at most 0.0095.
Values may be sent and summed in bfloat16 or wider, within the bound.
No kernel may reach another device: no remote copies, remote signals or barrier semaphores. Data moves between devices by JAX's collectives and lax.ppermute only.
A program may use at most 64 MiB of HBM per device.

```python
import jax
import jax.numpy as jnp
from jax import lax

D = 3072
HEADS = 24
HD = 128
GRID = 64
PROMPTS = 2
STEPS = 8
TXT = 512
IMG = 2048


def draw_query_gain(key, part):
    return 1.0 + jax.random.uniform(jax.random.fold_in(key, 11), (HD,), jnp.float32, -0.4, 0.4)


def draw_key_gain(key, part):
    return 1.0 + jax.random.uniform(jax.random.fold_in(key, 12), (2, HD), jnp.float32, -0.4, 0.4)


def draw_img_query(key, part):
    return jnp.clip(jax.random.normal(jax.random.fold_in(key, 31), (2, PROMPTS, IMG, D), jnp.float32), -6.0, 6.0).astype(jnp.bfloat16)


def draw_img_key(key, part):
    return jnp.clip(jax.random.normal(jax.random.fold_in(key, 32), (2, PROMPTS, IMG, D), jnp.float32), -6.0, 6.0).astype(jnp.bfloat16)


def draw_text_len(key, part):
    lengths = jax.random.randint(jax.random.fold_in(key, 41), (PROMPTS,), 1, TXT + 1)
    pick = jax.random.randint(jax.random.fold_in(key, 42), (), 0, PROMPTS)
    return jnp.where(jnp.arange(PROMPTS) == pick, TXT, lengths).astype(jnp.int32)


def raised(array, own_key, source, target, blocks, factor):
    def block_of(axis_at):
        return (jnp.arange(array.shape[axis_at]) // (array.shape[axis_at] // blocks)).reshape((-1,) + (1,) * (array.ndim - 1 - axis_at))

    near = jax.random.permutation(own_key, blocks)[block_of(target)]
    far = (block_of(target) + blocks // 2) % blocks
    return jnp.where((block_of(source) == near) | (block_of(source) == far), factor * array, array)


def steps_of(own_key, shape, split, low, high):
    gain, own = 1.0, jax.random.fold_in(own_key, 6)
    for position, blocks in split:
        draws = jnp.exp(jax.random.uniform(jax.random.fold_in(own, position), (blocks,), jnp.float32, low / len(split), high / len(split)))
        gain = gain * jnp.repeat(draws, shape[position] // blocks).reshape([-1 if axis == position else 1 for axis in range(len(shape))])
    return gain


def gaussian(rng, dims, deviation, most, cuts=(), held_as=jnp.bfloat16):
    entries = jax.random.normal(rng, dims, jnp.float32) * deviation
    if len(cuts) > 0:
        entries = steps_of(rng, dims, cuts, -0.22, 0.18) * entries
    return jnp.clip(entries, min=-most, max=most).astype(held_as)


def noise_with(own_key, extent, width, limit, split, heavy, dtype=jnp.bfloat16):
    array = width * jax.random.normal(own_key, extent, jnp.float32)
    if split:
        array = array * steps_of(own_key, extent, split, -0.22, 0.18)
    return jnp.clip(raised(array, jax.random.fold_in(own_key, 3), *heavy), -limit, limit).astype(dtype)


def setup_inputs(seed: int = 0) -> dict:
    streams_of = jax.random.split(jax.random.key(seed), 16)
    return {
        "img_hidden": gaussian(streams_of[0], (2, PROMPTS, IMG, D), 1.0, 6.0, ((0, 2), (2, 32), (3, 8))),
        "img_query": draw_img_query(jax.random.fold_in(streams_of[15], 71), 0),
        "img_key": draw_img_key(jax.random.fold_in(streams_of[15], 71), 0),
        "img_value": gaussian(streams_of[3], (2, PROMPTS, IMG, D), 1.0, 6.0, ((0, 2), (2, 32), (3, 8))),
        "txt_key": gaussian(streams_of[4], (2, PROMPTS, TXT, D), 1.0, 6.0, ((0, 2), (2, 32), (3, 8))),
        "txt_value": gaussian(streams_of[5], (2, PROMPTS, TXT, D), 1.0, 6.0, ((0, 2), (2, 32), (3, 8))),
        "query_gain": draw_query_gain(jax.random.fold_in(streams_of[15], 71), 0),
        "key_gain": draw_key_gain(jax.random.fold_in(streams_of[15], 71), 0),
        "gate": gaussian(streams_of[8], (2, PROMPTS, D), 1.0, 4.0, ((0, 2), (2, 8)), jnp.float32),
        "proj_weight": noise_with(streams_of[9], (D, D), D ** -0.5, 0.15625, ((0, 8),), (0, 1, 8, 2.0)),
        "proj_bias": gaussian(streams_of[10], (D,), 0.5, 3.0, ((0, 8),), jnp.float32),
        "guidance": jnp.clip(jax.random.uniform(streams_of[11], (PROMPTS,), jnp.float32, 1.5, 5.0), 1.5, 5.0),
        "text_len": draw_text_len(jax.random.fold_in(streams_of[15], 71), 0),
        "step_index": jax.random.randint(streams_of[13], (1,), 0, STEPS).astype(jnp.int32),
        "latent": gaussian(streams_of[14], (PROMPTS, IMG, D), 1.0, 6.0, ((0, 2), (1, 32), (2, 8))),
    }


def rope_angles(positions):
    first = HD // 8
    second = (HD - first) // 2
    freqs = 10000.0 ** (-jnp.arange(0, second, 2).astype(jnp.float32) / second)
    rows = (positions // GRID).astype(jnp.float32)
    cols = (positions % GRID).astype(jnp.float32)
    zeros = jnp.zeros((positions.shape[0], first // 2), jnp.float32)
    return jnp.concatenate([zeros, rows[:, None] * freqs, cols[:, None] * freqs], -1)

def rotate(values, angles):
    pairs = values.reshape(values.shape[:-1] + (HD // 2, 2))
    cosine = jnp.cos(angles)[:, None, :]
    sine = jnp.sin(angles)[:, None, :]
    first = pairs[..., 0] * cosine - pairs[..., 1] * sine
    second = pairs[..., 0] * sine + pairs[..., 1] * cosine
    return jnp.stack([first, second], -1).reshape(values.shape)

def normed(values, gain_row):
    heads = values.astype(jnp.float32).reshape(values.shape[0], HEADS, HD)
    return heads / jnp.sqrt(lax.optimization_barrier(jnp.mean(heads * heads, -1, keepdims=True)) + 1e-06) * gain_row

def one_half(hidden, query, key_img, value_img, key_txt, value_txt, query_gain, key_gain, gate_row, proj_weight, proj_bias, length):
    angles = rope_angles(jnp.arange(IMG))
    queries = rotate(normed(query, query_gain), angles).astype(jnp.bfloat16)
    keys_img = rotate(normed(key_img, key_gain[0]), angles).astype(jnp.bfloat16)
    keys_txt = normed(key_txt, key_gain[1]).astype(jnp.bfloat16)
    keys = jnp.concatenate([keys_txt, keys_img], 0)
    values = jnp.concatenate([value_txt, value_img], 0).reshape(TXT + IMG, HEADS, HD)
    live = jnp.concatenate([jnp.arange(TXT) < length, jnp.ones((IMG,), bool)])
    scores = jnp.einsum('qhd,khd->hqk', queries.astype(jnp.float32), keys.astype(jnp.float32)) * HD ** (-0.5)
    scores = jnp.where(live[None, None, :], scores, -1e+30)
    top = lax.optimization_barrier(jnp.max(scores, -1, keepdims=True))
    expo = jnp.exp(scores - top)
    total = lax.optimization_barrier(jnp.sum(expo, -1))
    weights = expo.astype(jnp.bfloat16)
    attn = jnp.einsum('hqk,khd->qhd', weights.astype(jnp.float32), values.astype(jnp.float32))
    attn = (attn / jnp.transpose(total)[:, :, None]).astype(jnp.bfloat16).reshape(IMG, D)
    proj = jnp.dot(attn, proj_weight, preferred_element_type=jnp.float32) + proj_bias
    return (hidden.astype(jnp.float32) + gate_row * proj).astype(jnp.bfloat16)

def plan(index):
    u_now = 1.0 - index.astype(jnp.float32) / STEPS
    u_next = 1.0 - (index + 1).astype(jnp.float32) / STEPS
    return 3.0 * u_next / (1.0 + 2.0 * u_next) - 3.0 * u_now / (1.0 + 2.0 * u_now)

def reference(img_hidden, img_query, img_key, img_value, txt_key, txt_value, query_gain, key_gain, gate, proj_weight, proj_bias, guidance, text_len, step_index, latent):
    step_size = plan(step_index[0])
    guided_rows = []
    next_rows = []
    for prompt in range(PROMPTS):
        outs = []
        for half in range(2):
            outs.append(one_half(img_hidden[half, prompt], img_query[half, prompt], img_key[half, prompt], img_value[half, prompt], txt_key[half, prompt], txt_value[half, prompt], query_gain, key_gain, gate[half, prompt], proj_weight, proj_bias, text_len[prompt]))
        cond = outs[0].astype(jnp.float32)
        uncond = outs[1].astype(jnp.float32)
        guided_f = uncond + guidance[prompt] * (cond - uncond)
        guided_rows.append(guided_f.astype(jnp.bfloat16))
        next_rows.append((latent[prompt].astype(jnp.float32) + step_size * guided_f).astype(jnp.bfloat16))
    return (jnp.stack(guided_rows, 0), jnp.stack(next_rows, 0))
```

```python
import functools

import jax
import jax.numpy as jnp
import numpy as np
from jax import lax
from jax.experimental import pallas as pl
from jax.experimental.pallas import tpu as pltpu
from jax.sharding import Mesh, PartitionSpec as P

HD = 128
GRID = 64
STEPS = 8
HPD = 3
W = HPD * HD
TQ = 64
TT = 16
TK = TQ + TT
NZ = 4
NS = 8
STAT = 8
BF = jnp.bfloat16
F32 = jnp.float32
VMEM_LIMIT = 48 * 1024 * 1024


def rope_tables():
    first = HD // 8
    second = (HD - first) // 2
    freqs = 10000.0 ** (-np.arange(0, second, 2).astype(np.float64) / second)
    n = freqs.shape[0]
    lane = np.arange(HD)
    pair = lane // 2
    sign = np.where(lane % 2 == 0, -1.0, 1.0)
    row_f = np.where((pair >= first // 2) & (pair < first // 2 + n), freqs[np.clip(pair - first // 2, 0, n - 1)], 0.0)
    col_f = np.where(pair >= first // 2 + n, freqs[np.clip(pair - first // 2 - n, 0, n - 1)], 0.0)
    rows = np.arange(32)[:, None] * row_f[None]
    cols = np.arange(GRID)[:, None] * col_f[None]
    return (
        np.stack([np.cos(rows), np.sin(rows) * sign]).astype(np.float32),
        np.stack([np.cos(cols), np.sin(cols) * sign]).astype(np.float32),
    )


def split3(x):
    hi = x.astype(BF)
    rest = x - hi.astype(F32)
    mid = rest.astype(BF)
    lo = (rest - mid.astype(F32)).astype(BF)
    return hi, mid, lo


def prepare_kernel(
    ids, q_ref, k_ref, v_ref, tk_ref, tv_ref, qg_ref, kg_ref, row_ref, col_ref, hid_ref, gate_ref, kv_out, q_out, side_out
):
    seq = ids[0]
    other = ids[1]
    lane = lax.broadcasted_iota(jnp.int32, (TQ, HD), 1)
    even = lane % 2 == 0
    in_row = lane < 72
    cos_t = jnp.where(in_row, row_ref[0, pl.ds(seq, 1), :], col_ref[0])
    sin_t = jnp.where(in_row, row_ref[1, pl.ds(seq, 1), :], col_ref[1])

    def normed(x, gain):
        x = x.astype(F32)
        return x * lax.rsqrt(jnp.mean(x * x, -1, keepdims=True) + 1e-06) * gain

    def rotated(x):
        swapped = jnp.where(even, pltpu.roll(x, HD - 1, 1), pltpu.roll(x, 1, 1))
        return x * cos_t + swapped * sin_t

    for p in range(2):
        for h in range(HPD):
            hs = slice(h * HD, (h + 1) * HD)
            q = rotated(normed(q_ref[p, :, hs], qg_ref[...])).astype(BF)
            k = rotated(normed(k_ref[p, :, hs], kg_ref[0:1])).astype(BF)
            t = normed(tk_ref[p, :, hs], kg_ref[1:2]).astype(BF)
            for z in range(NZ):
                q_out[p * NZ + z, :, hs] = q
                kv_out[p * NZ + z, 0, 0:TT, hs] = t
                kv_out[p * NZ + z, 0, TT:TK, hs] = k
        for z in range(NZ):
            kv_out[p * NZ + z, 1, 0:TT, :] = tv_ref[p]
            kv_out[p * NZ + z, 1, TT:TK, :] = v_ref[p]
    side_out[0:TQ, :] = hid_ref[other]
    hi, mid, lo = split3(gate_ref[pl.ds(other, 1), :])
    rows = lax.broadcasted_iota(jnp.int32, (8, W), 0)
    packed = jnp.where(rows == 0, hi.astype(F32), jnp.where(rows == 1, mid.astype(F32), lo.astype(F32)))
    side_out[TQ : TQ + 8, :] = packed.astype(BF)


def attend_kernel(q_ref, kv_ref, bias_ref, out_ref):
    scale = HD ** (-0.5) * 1.4426950408889634
    lane = lax.broadcasted_iota(jnp.int32, (NS * TQ, HD), 1)
    stats = jnp.zeros((NS * TQ, HD), F32)
    for h in range(HPD):
        hs = slice(h * HD, (h + 1) * HD)
        q = q_ref[:, :, hs].reshape(NS * TQ, HD)
        k = kv_ref[:, 0, :, hs].reshape(NS * TK, HD)
        v = kv_ref[:, 1, :, hs].reshape(NS * TK, HD)
        s = lax.dot_general(q, k, (((1,), (1,)), ((), ())), preferred_element_type=F32)
        s = s * scale + bias_ref[...]
        top = jnp.max(s, -1, keepdims=True)
        e = jnp.exp2(s - top)
        total = jnp.sum(e, -1, keepdims=True)
        o = jnp.dot(e.astype(BF), v, preferred_element_type=F32) / total
        out_ref[:, 0:TQ, hs] = o.astype(BF).reshape(NS, TQ, HD)
        lse = top + jnp.log2(total)
        hi = lse.astype(BF).astype(F32)
        stats = jnp.where(lane == h, hi, jnp.where(lane == HPD + h, lse - hi, stats))
    rows = jnp.transpose(stats)[0:STAT, :].astype(BF)
    for d in range(NS):
        a = (d // 2) * HD
        out_ref[d, TQ : TQ + STAT, 0:HD] = rows[:, a : a + HD]
        out_ref[d, TQ : TQ + STAT, HD:W] = jnp.zeros((STAT, W - HD), BF)


def project_kernel(ids, o_ref, w_ref, out_ref, attn_ref):
    odd = ids[0]
    stats = o_ref[:, TQ : TQ + STAT, 0:HD].astype(F32).reshape(NS * STAT, HD)
    cols = jnp.transpose(jnp.concatenate([stats, stats], 0))
    cols = jnp.where(odd == 0, cols[0:TQ], cols[TQ : 2 * TQ])
    for p in range(2):
        for h in range(HPD):
            hs = slice(h * HD, (h + 1) * HD)
            lses = []
            for z in range(NZ):
                at = (p * NZ + z) * STAT + h
                lses.append(cols[:, at : at + 1] + cols[:, at + HPD : at + HPD + 1])
            top = functools.reduce(jnp.maximum, lses)
            ws = [jnp.exp2(x - top) for x in lses]
            total = functools.reduce(jnp.add, ws)
            acc = jnp.zeros((TQ, HD), F32)
            for z in range(NZ):
                acc = acc + ws[z] * o_ref[p * NZ + z, 0:TQ, hs].astype(F32)
            attn_ref[p * TQ : (p + 1) * TQ, hs] = (acc / total).astype(BF)
    attn = attn_ref[...]
    for b in range(8):
        part = jnp.dot(attn, w_ref[:, b * W : (b + 1) * W], preferred_element_type=F32).astype(BF)
        out_ref[b] = part[0:TQ]
        out_ref[8 + b] = part[TQ : 2 * TQ]


def finish_kernel(ids, scal, part_ref, hid_ref, gate_ref, side_ref, bias_ref, lat_ref, guided_ref, next_ref):
    mine = ids[0]
    mine_f = mine.astype(F32)
    outs = []
    other_gate = (
        side_ref[TQ : TQ + 1, :].astype(F32) + side_ref[TQ + 1 : TQ + 2, :].astype(F32)
    ) + side_ref[TQ + 2 : TQ + 3, :].astype(F32)
    for g in range(2):
        acc = part_ref[g * 8].astype(F32)
        for b in range(1, 8):
            acc = acc + part_ref[g * 8 + b].astype(F32)
        own = mine == g
        hidden = jnp.where(own, hid_ref[mine].astype(F32), side_ref[0:TQ, :].astype(F32))
        gate = jnp.where(own, gate_ref[pl.ds(mine, 1), :], other_gate)
        outs.append((hidden + gate * (acc + bias_ref[...])).astype(BF).astype(F32))
    cond, uncond = outs
    guided = uncond + scal[0] * (cond - uncond)
    guided_ref[0] = guided.astype(BF)
    next_ref[0] = (lat_ref[0].astype(F32) + scal[1] * guided).astype(BF)


SMEM = functools.partial(pl.BlockSpec, memory_space=pltpu.SMEM)
VMEM = functools.partial(pl.BlockSpec, memory_space=pltpu.VMEM)


def call(kernel, outs, n_smem, n_vmem, name, scratch=()):
    return pl.pallas_call(
        kernel,
        out_shape=outs,
        in_specs=[SMEM()] * n_smem + [VMEM()] * n_vmem,
        out_specs=jax.tree.map(lambda _: VMEM(), outs),
        scratch_shapes=list(scratch),
        compiler_params=pltpu.CompilerParams(vmem_limit_bytes=VMEM_LIMIT),
        name=name,
    )


def shards(
    img_hidden,
    img_query,
    img_key,
    img_value,
    txt_key,
    txt_value,
    query_gain,
    key_gain,
    gate,
    proj_weight,
    proj_bias,
    guidance,
    text_len,
    step_index,
    latent,
):
    guide = lax.axis_index("g")
    xh = lax.axis_index("xh")
    z1 = lax.axis_index("z1")
    z0 = lax.axis_index("z0")
    seq = (xh * NZ + z1) * NZ + z0
    rows, cols = rope_tables()
    kv, q, side = call(
        prepare_kernel,
        (
            jax.ShapeDtypeStruct((NS, 2, TK, W), BF),
            jax.ShapeDtypeStruct((NS, TQ, W), BF),
            jax.ShapeDtypeStruct((TQ + 8, W), BF),
        ),
        1,
        11,
        "prepare",
    )(
        jnp.stack([seq, 1 - guide]),
        img_query[0],
        img_key[0],
        img_value[0],
        txt_key[0],
        txt_value[0],
        query_gain[None],
        key_gain,
        jnp.asarray(rows),
        jnp.asarray(cols),
        img_hidden[0],
        gate[0],
    )
    side = lax.ppermute(side, "g", [(0, 1), (1, 0)])
    q = lax.all_to_all(q, ("xh", "z1"), 0, 0, tiled=True)
    kv = lax.all_to_all(kv, ("xh", "z0"), 0, 0, tiled=True)

    src = jnp.arange(NS)
    src_seq = ((src // NZ) * NZ + z1) * NZ + src % NZ
    within = jnp.arange(TK)
    pos = src_seq[:, None] * TT + within[None, :]
    live = (within >= TT)[None, :] | (pos < text_len[xh])
    bias = jnp.where(live, 0.0, -1e30).astype(F32).reshape(1, NS * TK)
    out = call(attend_kernel, jax.ShapeDtypeStruct((NS, TQ + STAT, W), BF), 0, 3, "attend")(q, kv, bias)
    out = lax.all_to_all(out, ("xh", "z1"), 0, 0, tiled=True)
    part = call(
        project_kernel,
        jax.ShapeDtypeStruct((16, TQ, W), BF),
        1,
        2,
        "project",
        [pltpu.VMEM((2 * TQ, W), BF)],
    )((z1 % 2)[None], out, proj_weight)
    part = lax.all_to_all(part, ("g", "y", "c"), 0, 0, tiled=True)
    index = step_index[0]
    u_now = 1.0 - index.astype(F32) / STEPS
    u_next = 1.0 - (index + 1).astype(F32) / STEPS
    step = 3.0 * u_next / (1.0 + 2.0 * u_next) - 3.0 * u_now / (1.0 + 2.0 * u_now)
    shape = jax.ShapeDtypeStruct((1, TQ, W), BF)
    return call(finish_kernel, (shape, shape), 2, 6, "finish")(
        guide[None],
        jnp.stack([guidance[guide], step]),
        part,
        img_hidden[0],
        gate[0],
        side,
        proj_bias[None],
        latent,
    )


def solution(mesh):
    fine = Mesh(mesh.devices.reshape(2, 2, NZ, NZ, 4, 2), ("g", "xh", "z1", "z0", "y", "c"))
    seq = ("xh", "z1", "z0")
    blk = ("y", "c")
    act = P("g", None, seq, blk)
    return jax.shard_map(
        shards,
        mesh=fine,
        in_specs=(
            act,
            act,
            act,
            act,
            act,
            act,
            P(),
            P(),
            P("g", None, blk),
            P(blk, None),
            P(blk),
            P(),
            P(),
            P(),
            P("g", seq, blk),
        ),
        out_specs=(P("g", seq, blk), P("g", seq, blk)),
        check_vma=False,
    )
```

```python
import functools

import jax
import jax.numpy as jnp
import numpy as np
from jax import lax
from jax.experimental import pallas as pl
from jax.experimental.pallas import tpu as pltpu
from jax.sharding import Mesh, PartitionSpec as P

HD = 128
GRID = 64
STEPS = 8
HPD = 3
W = HPD * HD
TQ = 64
TT = 16
TK = TQ + TT
NZ = 4
NS = 8
STAT = 8
BF = jnp.bfloat16
F32 = jnp.float32
VMEM_LIMIT = 48 * 1024 * 1024


def rope_tables():
    first = HD // 8
    second = (HD - first) // 2
    freqs = 10000.0 ** (-np.arange(0, second, 2).astype(np.float64) / second)
    n = freqs.shape[0]
    lane = np.arange(HD)
    pair = lane // 2
    sign = np.where(lane % 2 == 0, -1.0, 1.0)
    row_f = np.where((pair >= first // 2) & (pair < first // 2 + n), freqs[np.clip(pair - first // 2, 0, n - 1)], 0.0)
    col_f = np.where(pair >= first // 2 + n, freqs[np.clip(pair - first // 2 - n, 0, n - 1)], 0.0)
    rows = np.arange(32)[:, None] * row_f[None]
    cols = np.arange(GRID)[:, None] * col_f[None]
    return (
        np.stack([np.cos(rows), np.sin(rows) * sign]).astype(np.float32),
        np.stack([np.cos(cols), np.sin(cols) * sign]).astype(np.float32),
    )


def split3(x):
    hi = x.astype(BF)
    rest = x - hi.astype(F32)
    mid = rest.astype(BF)
    lo = (rest - mid.astype(F32)).astype(BF)
    return hi, mid, lo


def prepare_kernel(
    ids, q_hbm, k_hbm, v_hbm, tk_hbm, tv_hbm, hid_hbm, gate_hbm, qg_hbm, kg_hbm, row_hbm, col_hbm,
    kv_out, q_out, side_out,
    q_ref, k_ref, v_ref, tk_ref, tv_ref, hid_ref, gate_ref, qg_ref, kg_ref, row_ref, col_ref, sems,
):
    seq = ids[0]
    other = ids[1]
    pairs = (
        (qg_hbm, qg_ref), (kg_hbm, kg_ref), (row_hbm.at[:, pl.ds(seq, 1)], row_ref), (col_hbm, col_ref), (q_hbm, q_ref),
        (k_hbm, k_ref), (tk_hbm, tk_ref), (v_hbm, v_ref), (tv_hbm, tv_ref), (hid_hbm.at[other], hid_ref), (gate_hbm, gate_ref),
    )
    copies = [pltpu.make_async_copy(src, dst, sems.at[i]) for i, (src, dst) in enumerate(pairs)]
    for copy in copies:
        copy.start()
    for copy in copies[:5]:
        copy.wait()
    lane = lax.broadcasted_iota(jnp.int32, (TQ, HD), 1)
    even = lane % 2 == 0
    in_row = lane < 72
    cos_t = jnp.where(in_row, row_ref[0], col_ref[0])
    sin_t = jnp.where(in_row, row_ref[1], col_ref[1])

    def normed(x, gain):
        x = x.astype(F32)
        return x * lax.rsqrt(jnp.mean(x * x, -1, keepdims=True) + 1e-06) * gain

    def rotated(x):
        swapped = jnp.where(even, pltpu.roll(x, HD - 1, 1), pltpu.roll(x, 1, 1))
        return x * cos_t + swapped * sin_t

    for p in range(2):
        for h in range(HPD):
            hs = slice(h * HD, (h + 1) * HD)
            q_out[p, :, hs] = rotated(normed(q_ref[p, :, hs], qg_ref[...])).astype(BF)
    copies[5].wait()
    copies[6].wait()
    for p in range(2):
        for h in range(HPD):
            hs = slice(h * HD, (h + 1) * HD)
            kv_out[p, 0, 0:TT, hs] = normed(tk_ref[p, :, hs], kg_ref[1:2]).astype(BF)
            kv_out[p, 0, TT:TK, hs] = rotated(normed(k_ref[p, :, hs], kg_ref[0:1])).astype(BF)
    for copy in copies[7:]:
        copy.wait()
    for p in range(2):
        kv_out[p, 1, 0:TT, :] = tv_ref[p]
        kv_out[p, 1, TT:TK, :] = v_ref[p]
    side_out[0:TQ, :] = hid_ref[...]
    hi, mid, lo = split3(gate_ref[pl.ds(other, 1), :])
    rows = lax.broadcasted_iota(jnp.int32, (8, W), 0)
    packed = jnp.where(rows == 0, hi.astype(F32), jnp.where(rows == 1, mid.astype(F32), lo.astype(F32)))
    side_out[TQ : TQ + 8, :] = packed.astype(BF)


def attend_kernel(q_ref, kv_ref, bias_ref, out_ref):
    scale = HD ** (-0.5) * 1.4426950408889634
    lane = lax.broadcasted_iota(jnp.int32, (NS * TQ, HD), 1)
    stats = jnp.zeros((NS * TQ, HD), F32)
    for h in range(HPD):
        hs = slice(h * HD, (h + 1) * HD)
        q = q_ref[:, :, hs].reshape(NS * TQ, HD)
        k = kv_ref[:, 0, :, hs].reshape(NS * TK, HD)
        v = kv_ref[:, 1, :, hs].reshape(NS * TK, HD)
        s = lax.dot_general(q, k, (((1,), (1,)), ((), ())), preferred_element_type=F32)
        s = s * scale + bias_ref[...]
        top = jnp.max(s, -1, keepdims=True)
        e = jnp.exp2(s - top)
        total = jnp.sum(e, -1, keepdims=True)
        o = jnp.dot(e.astype(BF), v, preferred_element_type=F32) / total
        o = o.astype(BF).reshape(NS, TQ, HD)
        for d in range(NS):
            out_ref[d, 0:TQ, hs] = o[(d % NZ) * 2 + d // NZ]
        lse = top + jnp.log2(total)
        hi = lse.astype(BF).astype(F32)
        stats = jnp.where(lane == h, hi, jnp.where(lane == HPD + h, lse - hi, stats))
    rows = jnp.transpose(stats)[0:STAT, :].astype(BF)
    for d in range(NS):
        a = (d % NZ) * HD
        out_ref[d, TQ : TQ + STAT, 0:HD] = rows[:, a : a + HD]
        out_ref[d, TQ : TQ + STAT, HD:W] = jnp.zeros((STAT, W - HD), BF)


def project_kernel(ids, o_ref, w_ref, out_ref, attn_ref):
    odd = ids[0]
    stats = o_ref[:, TQ : TQ + STAT, 0:HD].astype(F32).reshape(NS * STAT, HD)
    cols = jnp.transpose(jnp.concatenate([stats, stats], 0))
    cols = jnp.where(odd == 0, cols[0:TQ], cols[TQ : 2 * TQ])
    for p in range(2):
        for h in range(HPD):
            hs = slice(h * HD, (h + 1) * HD)
            lses = []
            for z in range(NZ):
                at = (p * NZ + z) * STAT + h
                lses.append(cols[:, at : at + 1] + cols[:, at + HPD : at + HPD + 1])
            top = functools.reduce(jnp.maximum, lses)
            ws = [jnp.exp2(x - top) for x in lses]
            total = functools.reduce(jnp.add, ws)
            acc = jnp.zeros((TQ, HD), F32)
            for z in range(NZ):
                acc = acc + ws[z] * o_ref[p * NZ + z, 0:TQ, hs].astype(F32)
            attn_ref[p * TQ : (p + 1) * TQ, hs] = (acc / total).astype(BF)
    attn = attn_ref[...]
    for b in range(8):
        part = jnp.dot(attn, w_ref[:, b * W : (b + 1) * W], preferred_element_type=F32).astype(BF)
        out_ref[b] = part[0:TQ]
        out_ref[8 + b] = part[TQ : 2 * TQ]


def finish_kernel(ids, scal, part_ref, hid_ref, gate_ref, side_ref, bias_ref, lat_ref, guided_ref, next_ref):
    mine = ids[0]
    mine_f = mine.astype(F32)
    outs = []
    other_gate = (
        side_ref[TQ : TQ + 1, :].astype(F32) + side_ref[TQ + 1 : TQ + 2, :].astype(F32)
    ) + side_ref[TQ + 2 : TQ + 3, :].astype(F32)
    for g in range(2):
        acc = part_ref[g * 8].astype(F32)
        for b in range(1, 8):
            acc = acc + part_ref[g * 8 + b].astype(F32)
        own = mine == g
        hidden = jnp.where(own, hid_ref[mine].astype(F32), side_ref[0:TQ, :].astype(F32))
        gate = jnp.where(own, gate_ref[pl.ds(mine, 1), :], other_gate)
        outs.append((hidden + gate * (acc + bias_ref[...])).astype(BF).astype(F32))
    cond, uncond = outs
    guided = uncond + scal[0] * (cond - uncond)
    guided_ref[0] = guided.astype(BF)
    next_ref[0] = (lat_ref[0].astype(F32) + scal[1] * guided).astype(BF)


SMEM = functools.partial(pl.BlockSpec, memory_space=pltpu.SMEM)
VMEM = functools.partial(pl.BlockSpec, memory_space=pltpu.VMEM)


def call(kernel, outs, n_smem, n_vmem, name, scratch=()):
    return pl.pallas_call(
        kernel,
        out_shape=outs,
        in_specs=[SMEM()] * n_smem + [VMEM()] * n_vmem,
        out_specs=jax.tree.map(lambda _: VMEM(), outs),
        scratch_shapes=list(scratch),
        compiler_params=pltpu.CompilerParams(vmem_limit_bytes=VMEM_LIMIT),
        name=name,
    )


def shards(
    img_hidden,
    img_query,
    img_key,
    img_value,
    txt_key,
    txt_value,
    query_gain,
    key_gain,
    gate,
    proj_weight,
    proj_bias,
    guidance,
    text_len,
    step_index,
    latent,
):
    guide = lax.axis_index("g")
    xh = lax.axis_index("xh")
    z1 = lax.axis_index("z1")
    z0 = lax.axis_index("z0")
    seq = (xh * NZ + z1) * NZ + z0
    rows, cols = rope_tables()
    kv, q, side = pl.pallas_call(
        prepare_kernel,
        out_shape=(
            jax.ShapeDtypeStruct((2, 2, TK, W), BF),
            jax.ShapeDtypeStruct((2, TQ, W), BF),
            jax.ShapeDtypeStruct((TQ + 8, W), BF),
        ),
        in_specs=[SMEM()] + [pl.BlockSpec(memory_space=pltpu.HBM)] * 11,
        out_specs=(VMEM(), VMEM(), VMEM()),
        scratch_shapes=[
            pltpu.VMEM((2, TQ, W), BF),
            pltpu.VMEM((2, TQ, W), BF),
            pltpu.VMEM((2, TQ, W), BF),
            pltpu.VMEM((2, TT, W), BF),
            pltpu.VMEM((2, TT, W), BF),
            pltpu.VMEM((TQ, W), BF),
            pltpu.VMEM((2, W), F32),
            pltpu.VMEM((1, HD), F32),
            pltpu.VMEM((2, HD), F32),
            pltpu.VMEM((2, 1, HD), F32),
            pltpu.VMEM((2, TQ, HD), F32),
            pltpu.SemaphoreType.DMA((11,)),
        ],
        compiler_params=pltpu.CompilerParams(vmem_limit_bytes=63 * 1024 * 1024),
        name="prepare",
    )(
        jnp.stack([seq, 1 - guide]),
        img_query[0],
        img_key[0],
        img_value[0],
        txt_key[0],
        txt_value[0],
        img_hidden[0],
        gate[0],
        query_gain[None],
        key_gain,
        jnp.asarray(rows),
        jnp.asarray(cols),
    )
    side = lax.ppermute(side, "g", [(0, 1), (1, 0)])
    q = lax.all_to_all(q, "xh", 0, 0, tiled=True)
    kv = lax.all_to_all(kv, "xh", 0, 0, tiled=True)
    q = lax.all_gather(q, "z1", axis=0, tiled=True)
    kv = lax.all_gather(kv, "z0", axis=0, tiled=True)

    src = jnp.arange(NS)
    src_seq = ((src % 2) * NZ + z1) * NZ + src // 2
    within = jnp.arange(TK)
    pos = src_seq[:, None] * TT + within[None, :]
    live = (within >= TT)[None, :] | (pos < text_len[xh])
    bias = jnp.where(live, 0.0, -1e30).astype(F32).reshape(1, NS * TK)
    out = call(attend_kernel, jax.ShapeDtypeStruct((NS, TQ + STAT, W), BF), 0, 3, "attend")(q, kv, bias)
    out = lax.all_to_all(out, ("xh", "z1"), 0, 0, tiled=True)
    part = call(
        project_kernel,
        jax.ShapeDtypeStruct((16, TQ, W), BF),
        1,
        2,
        "project",
        [pltpu.VMEM((2 * TQ, W), BF)],
    )(xh[None], out, proj_weight)
    part = lax.all_to_all(part, ("g", "y", "c"), 0, 0, tiled=True)
    index = step_index[0]
    u_now = 1.0 - index.astype(F32) / STEPS
    u_next = 1.0 - (index + 1).astype(F32) / STEPS
    step = 3.0 * u_next / (1.0 + 2.0 * u_next) - 3.0 * u_now / (1.0 + 2.0 * u_now)
    shape = jax.ShapeDtypeStruct((1, TQ, W), BF)
    return call(finish_kernel, (shape, shape), 2, 6, "finish")(
        guide[None],
        jnp.stack([guidance[guide], step]),
        part,
        img_hidden[0],
        gate[0],
        side,
        proj_bias[None],
        latent,
    )


def solution(mesh):
    fine = Mesh(mesh.devices.reshape(2, 2, NZ, NZ, 4, 2), ("g", "xh", "z1", "z0", "y", "c"))
    seq = ("xh", "z1", "z0")
    blk = ("y", "c")
    act = P("g", None, seq, blk)
    return jax.shard_map(
        shards,
        mesh=fine,
        in_specs=(
            act,
            act,
            act,
            act,
            act,
            act,
            P(),
            P(),
            P("g", None, blk),
            P(blk, None),
            P(blk),
            P(),
            P(),
            P(),
            P("g", seq, blk),
        ),
        out_specs=(P("g", seq, blk), P("g", seq, blk)),
        check_vma=False,
    )
```

```python
import functools

import jax
import jax.numpy as jnp
import numpy as np
from jax import lax
from jax.experimental import pallas as pl
from jax.experimental.pallas import tpu as pltpu
from jax.sharding import Mesh, PartitionSpec as P

HD = 128
GRID = 64
STEPS = 8
HPD = 3
W = HPD * HD
TQ = 64
TT = 16
TK = TQ + TT
NZ = 4
NS = 8
STAT = 8
BF = jnp.bfloat16
F32 = jnp.float32
VMEM_LIMIT = 48 * 1024 * 1024


def rope_tables():
    first = HD // 8
    second = (HD - first) // 2
    freqs = 10000.0 ** (-np.arange(0, second, 2).astype(np.float64) / second)
    n = freqs.shape[0]
    lane = np.arange(HD)
    pair = lane // 2
    sign = np.where(lane % 2 == 0, -1.0, 1.0)
    row_f = np.where((pair >= first // 2) & (pair < first // 2 + n), freqs[np.clip(pair - first // 2, 0, n - 1)], 0.0)
    col_f = np.where(pair >= first // 2 + n, freqs[np.clip(pair - first // 2 - n, 0, n - 1)], 0.0)
    rows = np.arange(32)[:, None] * row_f[None]
    cols = np.arange(GRID)[:, None] * col_f[None]
    return (
        np.stack([np.cos(rows), np.sin(rows) * sign]).astype(np.float32),
        np.stack([np.cos(cols), np.sin(cols) * sign]).astype(np.float32),
    )


def split3(x):
    hi = x.astype(BF)
    rest = x - hi.astype(F32)
    mid = rest.astype(BF)
    lo = (rest - mid.astype(F32)).astype(BF)
    return hi, mid, lo


def rope_of(row_ref, col_ref):
    in_row = lax.broadcasted_iota(jnp.int32, (TQ, HD), 1) < 72
    return jnp.where(in_row, row_ref[0], col_ref[0]), jnp.where(in_row, row_ref[1], col_ref[1])


def normed(x, gain):
    x = x.astype(F32)
    return x * lax.rsqrt(jnp.mean(x * x, -1, keepdims=True) + 1e-06) * gain


def rotated(x, table):
    even = lax.broadcasted_iota(jnp.int32, (TQ, HD), 1) % 2 == 0
    swapped = jnp.where(even, pltpu.roll(x, HD - 1, 1), pltpu.roll(x, 1, 1))
    return x * table[0] + swapped * table[1]


def start_all(pairs, sems):
    copies = [pltpu.make_async_copy(src, dst, sems.at[i]) for i, (src, dst) in enumerate(pairs)]
    for copy in copies:
        copy.start()
    return copies


def keys_kernel(
    ids, k_hbm, v_hbm, tk_hbm, tv_hbm, kg_hbm, row_hbm, col_hbm,
    kv_out,
    k_ref, v_ref, tk_ref, tv_ref, kg_ref, row_ref, col_ref, sems,
):
    copies = start_all(
        ((kg_hbm, kg_ref), (tk_hbm, tk_ref), (row_hbm.at[:, pl.ds(ids[0], 1)], row_ref), (col_hbm, col_ref), (k_hbm, k_ref), (v_hbm, v_ref), (tv_hbm, tv_ref)),
        sems,
    )
    for copy in copies[:5]:
        copy.wait()
    table = rope_of(row_ref, col_ref)
    for p in range(2):
        for h in range(HPD):
            hs = slice(h * HD, (h + 1) * HD)
            kv_out[p, 0, 0:TT, hs] = normed(tk_ref[p, :, hs], kg_ref[1:2]).astype(BF)
            kv_out[p, 0, TT:TK, hs] = rotated(normed(k_ref[p, :, hs], kg_ref[0:1]), table).astype(BF)
    for copy in copies[5:]:
        copy.wait()
    for p in range(2):
        kv_out[p, 1, 0:TT, :] = tv_ref[p]
        kv_out[p, 1, TT:TK, :] = v_ref[p]


def queries_kernel(
    ids, q_hbm, hid_hbm, gate_hbm, qg_hbm, row_hbm, col_hbm,
    q_out, side_out,
    q_ref, hid_ref, gate_ref, qg_ref, row_ref, col_ref, sems,
):
    other = ids[1]
    copies = start_all(
        ((qg_hbm, qg_ref), (row_hbm.at[:, pl.ds(ids[0], 1)], row_ref), (col_hbm, col_ref), (q_hbm, q_ref), (hid_hbm.at[other], hid_ref), (gate_hbm, gate_ref)),
        sems,
    )
    for copy in copies[:4]:
        copy.wait()
    table = rope_of(row_ref, col_ref)
    for p in range(2):
        for h in range(HPD):
            hs = slice(h * HD, (h + 1) * HD)
            q = rotated(normed(q_ref[p, :, hs], qg_ref[...]), table).astype(BF)
            for z in range(NZ):
                q_out[p * NZ + z, :, hs] = q
    for copy in copies[4:]:
        copy.wait()
    side_out[0:TQ, :] = hid_ref[...]
    hi, mid, lo = split3(gate_ref[pl.ds(other, 1), :])
    rows = lax.broadcasted_iota(jnp.int32, (8, W), 0)
    packed = jnp.where(rows == 0, hi.astype(F32), jnp.where(rows == 1, mid.astype(F32), lo.astype(F32)))
    side_out[TQ : TQ + 8, :] = packed.astype(BF)


def attend_kernel(q_ref, kv_ref, bias_ref, out_ref):
    scale = HD ** (-0.5) * 1.4426950408889634
    lane = lax.broadcasted_iota(jnp.int32, (NS * TQ, HD), 1)
    stats = jnp.zeros((NS * TQ, HD), F32)
    for h in range(HPD):
        hs = slice(h * HD, (h + 1) * HD)
        q = q_ref[:, :, hs].reshape(NS * TQ, HD)
        k = kv_ref[:, 0, :, hs].reshape(NS * TK, HD)
        v = kv_ref[:, 1, :, hs].reshape(NS * TK, HD)
        s = lax.dot_general(q, k, (((1,), (1,)), ((), ())), preferred_element_type=F32)
        s = s * scale + bias_ref[...]
        top = jnp.max(s, -1, keepdims=True)
        e = jnp.exp2(s - top)
        total = jnp.sum(e, -1, keepdims=True)
        o = jnp.dot(e.astype(BF), v, preferred_element_type=F32) / total
        o = o.astype(BF).reshape(NS, TQ, HD)
        for d in range(NS):
            out_ref[d, 0:TQ, hs] = o[d]
        lse = top + jnp.log2(total)
        hi = lse.astype(BF).astype(F32)
        stats = jnp.where(lane == h, hi, jnp.where(lane == HPD + h, lse - hi, stats))
    rows = jnp.transpose(stats)[0:STAT, :].astype(BF)
    for d in range(NS):
        a = (d // 2) * HD
        out_ref[d, TQ : TQ + STAT, 0:HD] = rows[:, a : a + HD]
        out_ref[d, TQ : TQ + STAT, HD:W] = jnp.zeros((STAT, W - HD), BF)


def project_kernel(ids, o_ref, w_ref, out_ref, attn_ref):
    odd = ids[0]
    stats = o_ref[:, TQ : TQ + STAT, 0:HD].astype(F32).reshape(NS * STAT, HD)
    cols = jnp.transpose(jnp.concatenate([stats, stats], 0))
    cols = jnp.where(odd == 0, cols[0:TQ], cols[TQ : 2 * TQ])
    for p in range(2):
        for h in range(HPD):
            hs = slice(h * HD, (h + 1) * HD)
            lses = []
            for z in range(NZ):
                at = (p * NZ + z) * STAT + h
                lses.append(cols[:, at : at + 1] + cols[:, at + HPD : at + HPD + 1])
            top = functools.reduce(jnp.maximum, lses)
            ws = [jnp.exp2(x - top) for x in lses]
            total = functools.reduce(jnp.add, ws)
            acc = jnp.zeros((TQ, HD), F32)
            for z in range(NZ):
                acc = acc + ws[z] * o_ref[p * NZ + z, 0:TQ, hs].astype(F32)
            attn_ref[p * TQ : (p + 1) * TQ, hs] = (acc / total).astype(BF)
    attn = attn_ref[...]
    for b in range(8):
        part = jnp.dot(attn, w_ref[:, b * W : (b + 1) * W], preferred_element_type=F32).astype(BF)
        out_ref[b] = part[0:TQ]
        out_ref[8 + b] = part[TQ : 2 * TQ]


def finish_kernel(ids, scal, part_ref, hid_ref, gate_ref, side_ref, bias_ref, lat_ref, guided_ref, next_ref):
    mine = ids[0]
    mine_f = mine.astype(F32)
    outs = []
    other_gate = (
        side_ref[TQ : TQ + 1, :].astype(F32) + side_ref[TQ + 1 : TQ + 2, :].astype(F32)
    ) + side_ref[TQ + 2 : TQ + 3, :].astype(F32)
    for g in range(2):
        acc = part_ref[g * 8].astype(F32)
        for b in range(1, 8):
            acc = acc + part_ref[g * 8 + b].astype(F32)
        own = mine == g
        hidden = jnp.where(own, hid_ref[mine].astype(F32), side_ref[0:TQ, :].astype(F32))
        gate = jnp.where(own, gate_ref[pl.ds(mine, 1), :], other_gate)
        outs.append((hidden + gate * (acc + bias_ref[...])).astype(BF).astype(F32))
    cond, uncond = outs
    guided = uncond + scal[0] * (cond - uncond)
    guided_ref[0] = guided.astype(BF)
    next_ref[0] = (lat_ref[0].astype(F32) + scal[1] * guided).astype(BF)


SMEM = functools.partial(pl.BlockSpec, memory_space=pltpu.SMEM)
VMEM = functools.partial(pl.BlockSpec, memory_space=pltpu.VMEM)


def call(kernel, outs, n_smem, n_vmem, name, scratch=()):
    return pl.pallas_call(
        kernel,
        out_shape=outs,
        in_specs=[SMEM()] * n_smem + [VMEM()] * n_vmem,
        out_specs=jax.tree.map(lambda _: VMEM(), outs),
        scratch_shapes=list(scratch),
        compiler_params=pltpu.CompilerParams(vmem_limit_bytes=VMEM_LIMIT),
        name=name,
    )


def from_hbm(kernel, outs, n_hbm, name, scratch):
    return pl.pallas_call(
        kernel,
        out_shape=outs,
        in_specs=[SMEM()] + [pl.BlockSpec(memory_space=pltpu.HBM)] * n_hbm,
        out_specs=jax.tree.map(lambda _: VMEM(), outs),
        scratch_shapes=scratch + [pltpu.SemaphoreType.DMA((n_hbm,))],
        compiler_params=pltpu.CompilerParams(vmem_limit_bytes=63 * 1024 * 1024),
        name=name,
    )


def shards(
    img_hidden,
    img_query,
    img_key,
    img_value,
    txt_key,
    txt_value,
    query_gain,
    key_gain,
    gate,
    proj_weight,
    proj_bias,
    guidance,
    text_len,
    step_index,
    latent,
):
    guide = lax.axis_index("g")
    xh = lax.axis_index("xh")
    z1 = lax.axis_index("z1")
    z0 = lax.axis_index("z0")
    seq = (xh * NZ + z1) * NZ + z0
    rows, cols = rope_tables()
    ids = jnp.stack([seq, 1 - guide])
    row_t = jnp.asarray(rows)
    col_t = jnp.asarray(cols)
    rope_scratch = [pltpu.VMEM((2, 1, HD), F32), pltpu.VMEM((2, TQ, HD), F32)]
    kv = from_hbm(
        keys_kernel,
        jax.ShapeDtypeStruct((2, 2, TK, W), BF),
        7,
        "keys",
        [
            pltpu.VMEM((2, TQ, W), BF),
            pltpu.VMEM((2, TQ, W), BF),
            pltpu.VMEM((2, TT, W), BF),
            pltpu.VMEM((2, TT, W), BF),
            pltpu.VMEM((2, HD), F32),
        ]
        + rope_scratch,
    )(ids, img_key[0], img_value[0], txt_key[0], txt_value[0], key_gain, row_t, col_t)
    kv = lax.all_to_all(kv, "xh", 0, 0, tiled=True)
    q, side = from_hbm(
        queries_kernel,
        (jax.ShapeDtypeStruct((NS, TQ, W), BF), jax.ShapeDtypeStruct((TQ + 8, W), BF)),
        6,
        "queries",
        [pltpu.VMEM((2, TQ, W), BF), pltpu.VMEM((TQ, W), BF), pltpu.VMEM((2, W), F32), pltpu.VMEM((1, HD), F32)] + rope_scratch,
    )(ids, img_query[0], img_hidden[0], gate[0], query_gain[None], row_t, col_t)
    side = lax.ppermute(side, "g", [(0, 1), (1, 0)])
    q, kv = lax.optimization_barrier((q, kv))
    q = lax.all_to_all(q, ("xh", "z0"), 0, 0, tiled=True)
    kv = lax.all_gather(kv, "z1", axis=0, tiled=True)

    src = jnp.arange(NS)
    src_seq = ((src % 2) * NZ + src // 2) * NZ + z0
    within = jnp.arange(TK)
    pos = src_seq[:, None] * TT + within[None, :]
    live = (within >= TT)[None, :] | (pos < text_len[xh])
    bias = jnp.where(live, 0.0, -1e30).astype(F32).reshape(1, NS * TK)
    out = call(attend_kernel, jax.ShapeDtypeStruct((NS, TQ + STAT, W), BF), 0, 3, "attend")(q, kv, bias)
    out = lax.all_to_all(out, ("xh", "z0"), 0, 0, tiled=True)
    part = call(
        project_kernel,
        jax.ShapeDtypeStruct((16, TQ, W), BF),
        1,
        2,
        "project",
        [pltpu.VMEM((2 * TQ, W), BF)],
    )((z0 & 1)[None], out, proj_weight)
    part = lax.all_to_all(part, ("g", "y", "c"), 0, 0, tiled=True)
    index = step_index[0]
    u_now = 1.0 - index.astype(F32) / STEPS
    u_next = 1.0 - (index + 1).astype(F32) / STEPS
    step = 3.0 * u_next / (1.0 + 2.0 * u_next) - 3.0 * u_now / (1.0 + 2.0 * u_now)
    shape = jax.ShapeDtypeStruct((1, TQ, W), BF)
    return call(finish_kernel, (shape, shape), 2, 6, "finish")(
        guide[None],
        jnp.stack([guidance[guide], step]),
        part,
        img_hidden[0],
        gate[0],
        side,
        proj_bias[None],
        latent,
    )


def solution(mesh):
    fine = Mesh(mesh.devices.reshape(2, 2, NZ, NZ, 4, 2), ("g", "xh", "z1", "z0", "y", "c"))
    seq = ("xh", "z1", "z0")
    blk = ("y", "c")
    act = P("g", None, seq, blk)
    return jax.shard_map(
        shards,
        mesh=fine,
        in_specs=(
            act,
            act,
            act,
            act,
            act,
            act,
            P(),
            P(),
            P("g", None, blk),
            P(blk, None),
            P(blk),
            P(),
            P(),
            P(),
            P("g", seq, blk),
        ),
        out_specs=(P("g", seq, blk), P("g", seq, blk)),
        check_vma=False,
    )
```

```python
import functools

import jax
import jax.numpy as jnp
import numpy as np
from jax import lax
from jax.experimental import pallas as pl
from jax.experimental.pallas import tpu as pltpu
from jax.sharding import Mesh, PartitionSpec as P

HD = 128
GRID = 64
STEPS = 8
HPD = 3
W = HPD * HD
TQ = 64
TT = 16
TK = TQ + TT
NZ = 4
NS = 8
STAT = 8
BF = jnp.bfloat16
F32 = jnp.float32
VMEM_LIMIT = 48 * 1024 * 1024


def rope_tables():
    first = HD // 8
    second = (HD - first) // 2
    freqs = 10000.0 ** (-np.arange(0, second, 2).astype(np.float64) / second)
    n = freqs.shape[0]
    lane = np.arange(HD)
    pair = lane // 2
    sign = np.where(lane % 2 == 0, -1.0, 1.0)
    row_f = np.where((pair >= first // 2) & (pair < first // 2 + n), freqs[np.clip(pair - first // 2, 0, n - 1)], 0.0)
    col_f = np.where(pair >= first // 2 + n, freqs[np.clip(pair - first // 2 - n, 0, n - 1)], 0.0)
    rows = np.arange(32)[:, None] * row_f[None]
    cols = np.arange(GRID)[:, None] * col_f[None]
    return (
        np.stack([np.cos(rows), np.sin(rows) * sign]).astype(np.float32),
        np.stack([np.cos(cols), np.sin(cols) * sign]).astype(np.float32),
    )


def split3(x):
    hi = x.astype(BF)
    rest = x - hi.astype(F32)
    mid = rest.astype(BF)
    lo = (rest - mid.astype(F32)).astype(BF)
    return hi, mid, lo


def rope_of(row_ref, col_ref):
    in_row = lax.broadcasted_iota(jnp.int32, (TQ, HD), 1) < 72
    return jnp.where(in_row, row_ref[0], col_ref[0]), jnp.where(in_row, row_ref[1], col_ref[1])


def normed(x, gain):
    x = x.astype(F32)
    return x * lax.rsqrt(jnp.mean(x * x, -1, keepdims=True) + 1e-06) * gain


def rotated(x, table):
    even = lax.broadcasted_iota(jnp.int32, (TQ, HD), 1) % 2 == 0
    swapped = jnp.where(even, pltpu.roll(x, HD - 1, 1), pltpu.roll(x, 1, 1))
    return x * table[0] + swapped * table[1]


def start_all(pairs, sems):
    copies = [pltpu.make_async_copy(src, dst, sems.at[i]) for i, (src, dst) in enumerate(pairs)]
    for copy in copies:
        copy.start()
    return copies


def keys_kernel(
    seq_id, xh_id, k_hbm, v_hbm, tk_hbm, tv_hbm, kg_hbm, row_hbm, col_hbm,
    keep_out, send_out,
    k_ref, v_ref, tk_ref, tv_ref, kg_ref, row_ref, col_ref, sems,
):
    rows = row_hbm.at[:, pl.ds(seq_id[0], 1)]
    copies = start_all(
        ((rows, row_ref), (col_hbm, col_ref), (kg_hbm, kg_ref), (tk_hbm, tk_ref), (k_hbm, k_ref), (v_hbm, v_ref), (tv_hbm, tv_ref)),
        sems,
    )
    for copy in copies[:5]:
        copy.wait()
    table = rope_of(row_ref, col_ref)
    own = xh_id[0]
    for out, p in ((send_out, 1 - own), (keep_out, own)):
        for h in range(HPD):
            hs = slice(h * HD, (h + 1) * HD)
            out[0, 0:TT, hs] = normed(tk_ref[p, :, hs], kg_ref[1:2]).astype(BF)
            out[0, TT:TK, hs] = rotated(normed(k_ref[p, :, hs], kg_ref[0:1]), table).astype(BF)
    for copy in copies[5:]:
        copy.wait()
    for out, p in ((send_out, 1 - own), (keep_out, own)):
        out[1, 0:TT, :] = tv_ref[p]
        out[1, TT:TK, :] = v_ref[p]


def queries_kernel(
    seq_id, guide_id, q_hbm, hid_hbm, gate_hbm, qg_hbm, row_hbm, col_hbm, after_hbm,
    q_out, side_out,
    q_ref, hid_ref, gate_ref, qg_ref, row_ref, col_ref, sems,
):
    other = 1 - guide_id[0]
    rows = row_hbm.at[:, pl.ds(seq_id[0], 1)]
    copies = start_all(
        ((rows, row_ref), (col_hbm, col_ref), (qg_hbm, qg_ref), (q_hbm, q_ref), (hid_hbm.at[other], hid_ref), (gate_hbm, gate_ref)),
        sems,
    )
    for copy in copies[:4]:
        copy.wait()
    table = rope_of(row_ref, col_ref)
    for p in range(2):
        for h in range(HPD):
            hs = slice(h * HD, (h + 1) * HD)
            q = rotated(normed(q_ref[p, :, hs], qg_ref[...]), table).astype(BF)
            for z in range(NZ):
                q_out[p * NZ + z, :, hs] = q
    for copy in copies[4:]:
        copy.wait()
    side_out[0:TQ, :] = hid_ref[...]
    hi, mid, lo = split3(gate_ref[pl.ds(other, 1), :])
    rows = lax.broadcasted_iota(jnp.int32, (8, W), 0)
    packed = jnp.where(rows == 0, hi.astype(F32), jnp.where(rows == 1, mid.astype(F32), lo.astype(F32)))
    side_out[TQ : TQ + 8, :] = packed.astype(BF)


def attend_kernel(xh_id, z0_id, len_ref, q_ref, kv_ref, out_hbm, out_ref, sems):
    scale = HD ** (-0.5) * 1.4426950408889634
    own = xh_id[0]
    at = lax.broadcasted_iota(jnp.int32, (1, NS * TK), 1)
    block = jnp.zeros_like(at)
    for i in range(1, NS):
        block = block + (at >= i * TK).astype(jnp.int32)
    within = at - block * TK
    from_own = (block & 1) == 0
    seq = (jnp.where(from_own, own, 1 - own) * NZ + (block >> 1)) * NZ + z0_id[0]
    dead = (within < TT) & (seq * TT + within >= len_ref[own])
    bias = jnp.where(dead, -1e30, 0.0)
    lane = lax.broadcasted_iota(jnp.int32, (NS * TQ, HD), 1)
    stats = jnp.zeros((NS * TQ, HD), F32)
    copies = []
    for h in range(HPD):
        hs = slice(h * HD, (h + 1) * HD)
        q = q_ref[:, :, hs].reshape(NS * TQ, HD)
        k = kv_ref[:, :, 0, :, hs].reshape(NS * TK, HD)
        v = kv_ref[:, :, 1, :, hs].reshape(NS * TK, HD)
        s = lax.dot_general(q, k, (((1,), (1,)), ((), ())), preferred_element_type=F32)
        s = s * scale + bias
        top = jnp.max(s, -1, keepdims=True)
        e = jnp.exp2(s - top)
        total = jnp.sum(e, -1, keepdims=True)
        o = jnp.dot(e.astype(BF), v, preferred_element_type=F32) / total
        out_ref[:, 0:TQ, hs] = o.astype(BF).reshape(NS, TQ, HD)
        copy = pltpu.make_async_copy(out_ref.at[:, 0:TQ, hs], out_hbm.at[:, 0:TQ, hs], sems.at[h])
        copy.start()
        copies.append(copy)
        lse = top + jnp.log2(total)
        hi = lse.astype(BF).astype(F32)
        stats = jnp.where(lane == h, hi, jnp.where(lane == HPD + h, lse - hi, stats))
    rows = jnp.transpose(stats)[0:STAT, :].astype(BF)
    for d in range(NS):
        a = (d // 2) * HD
        out_ref[d, TQ : TQ + STAT, 0:HD] = rows[:, a : a + HD]
        out_ref[d, TQ : TQ + STAT, HD:W] = jnp.zeros((STAT, W - HD), BF)
    copy = pltpu.make_async_copy(out_ref.at[:, TQ : TQ + STAT, :], out_hbm.at[:, TQ : TQ + STAT, :], sems.at[HPD])
    copy.start()
    copies.append(copy)
    for copy in copies:
        copy.wait()


def project_kernel(ids, o_ref, w_ref, out_hbm, attn_ref, out_ref, sems):
    odd = ids[0]
    stats = o_ref[:, TQ : TQ + STAT, 0:HD].astype(F32).reshape(NS * STAT, HD)
    cols = jnp.transpose(jnp.concatenate([stats, stats], 0))
    cols = jnp.where(odd == 0, cols[0:TQ], cols[TQ : 2 * TQ])
    for p in range(2):
        for h in range(HPD):
            hs = slice(h * HD, (h + 1) * HD)
            lses = []
            for z in range(NZ):
                at = (p * NZ + z) * STAT + h
                lses.append(cols[:, at : at + 1] + cols[:, at + HPD : at + HPD + 1])
            top = functools.reduce(jnp.maximum, lses)
            ws = [jnp.exp2(x - top) for x in lses]
            total = functools.reduce(jnp.add, ws)
            acc = jnp.zeros((TQ, HD), F32)
            for z in range(NZ):
                acc = acc + ws[z] * o_ref[p * NZ + z, 0:TQ, hs].astype(F32)
            attn_ref[p * TQ : (p + 1) * TQ, hs] = (acc / total).astype(BF)
    attn = attn_ref[...]
    copies = []
    for b in range(8):
        part = jnp.dot(attn, w_ref[:, b * W : (b + 1) * W], preferred_element_type=F32).astype(BF)
        out_ref[0, b] = part[0:TQ]
        out_ref[1, b] = part[TQ : 2 * TQ]
        copy = pltpu.make_async_copy(out_ref.at[:, b], out_hbm.at[:, b], sems.at[b])
        copy.start()
        copies.append(copy)
    for copy in copies:
        copy.wait()


def finish_kernel(ids, scal, part_ref, hid_ref, gate_ref, side_ref, bias_ref, lat_ref, guided_ref, next_ref):
    mine = ids[0]
    mine_f = mine.astype(F32)
    outs = []
    other_gate = (
        side_ref[TQ : TQ + 1, :].astype(F32) + side_ref[TQ + 1 : TQ + 2, :].astype(F32)
    ) + side_ref[TQ + 2 : TQ + 3, :].astype(F32)
    for g in range(2):
        acc = part_ref[g * 8].astype(F32)
        for b in range(1, 8):
            acc = acc + part_ref[g * 8 + b].astype(F32)
        own = mine == g
        hidden = jnp.where(own, hid_ref[mine].astype(F32), side_ref[0:TQ, :].astype(F32))
        gate = jnp.where(own, gate_ref[pl.ds(mine, 1), :], other_gate)
        outs.append((hidden + gate * (acc + bias_ref[...])).astype(BF).astype(F32))
    cond, uncond = outs
    guided = uncond + scal[0] * (cond - uncond)
    guided_ref[0] = guided.astype(BF)
    next_ref[0] = (lat_ref[0].astype(F32) + scal[1] * guided).astype(BF)


SMEM = functools.partial(pl.BlockSpec, memory_space=pltpu.SMEM)
VMEM = functools.partial(pl.BlockSpec, memory_space=pltpu.VMEM)
HBM = functools.partial(pl.BlockSpec, memory_space=pltpu.HBM)


def call(kernel, outs, ins, out_specs, name, scratch=(), limit=VMEM_LIMIT):
    return pl.pallas_call(
        kernel,
        out_shape=outs,
        in_specs=ins,
        out_specs=out_specs,
        scratch_shapes=list(scratch),
        compiler_params=pltpu.CompilerParams(vmem_limit_bytes=limit),
        name=name,
    )


def shards(
    img_hidden,
    img_query,
    img_key,
    img_value,
    txt_key,
    txt_value,
    query_gain,
    key_gain,
    gate,
    proj_weight,
    proj_bias,
    guidance,
    text_len,
    step_index,
    latent,
):
    guide = lax.axis_index("g")
    xh = lax.axis_index("xh")
    z1 = lax.axis_index("z1")
    z0 = lax.axis_index("z0")
    seq = (xh * NZ + z1) * NZ + z0
    rows, cols = rope_tables()
    kv_shape = jax.ShapeDtypeStruct((2, TK, W), BF)
    row_t = jnp.asarray(rows)
    col_t = jnp.asarray(cols)
    rope_scratch = [pltpu.VMEM((2, 1, HD), F32), pltpu.VMEM((2, TQ, HD), F32)]
    keep, send = call(
        keys_kernel,
        (kv_shape, kv_shape),
        [SMEM()] * 2 + [HBM()] * 7,
        (VMEM(),) * 2,
        "keys",
        [
            pltpu.VMEM((2, TQ, W), BF),
            pltpu.VMEM((2, TQ, W), BF),
            pltpu.VMEM((2, TT, W), BF),
            pltpu.VMEM((2, TT, W), BF),
            pltpu.VMEM((2, HD), F32),
            *rope_scratch,
            pltpu.SemaphoreType.DMA((7,)),
        ],
        63 * 1024 * 1024,
    )(seq[None], xh[None], img_key[0], img_value[0], txt_key[0], txt_value[0], key_gain, row_t, col_t)
    swap = [(0, 1), (1, 0)]
    got = lax.ppermute(send, "xh", swap)
    q, side = call(
        queries_kernel,
        (jax.ShapeDtypeStruct((NS, TQ, W), BF), jax.ShapeDtypeStruct((TQ + 8, W), BF)),
        [SMEM()] * 2 + [HBM()] * 7,
        (VMEM(),) * 2,
        "queries",
        [
            pltpu.VMEM((2, TQ, W), BF),
            pltpu.VMEM((TQ, W), BF),
            pltpu.VMEM((2, W), F32),
            pltpu.VMEM((1, HD), F32),
            *rope_scratch,
            pltpu.SemaphoreType.DMA((6,)),
        ],
        63 * 1024 * 1024,
    )(seq[None], guide[None], img_query[0], img_hidden[0], gate[0], query_gain[None], row_t, col_t, send)
    side = lax.ppermute(side, "g", swap)
    q, got = lax.optimization_barrier((q, got))
    q = lax.all_to_all(q, ("xh", "z0"), 0, 0, tiled=True)
    kv = lax.all_gather(jnp.stack([keep, got]), "z1", axis=0)

    out = call(
        attend_kernel,
        jax.ShapeDtypeStruct((NS, TQ + STAT, W), BF),
        [SMEM()] * 3 + [VMEM()] * 2,
        HBM(),
        "attend",
        [pltpu.VMEM((NS, TQ + STAT, W), BF), pltpu.SemaphoreType.DMA((HPD + 1,))],
    )(xh[None], z0[None], text_len, q, kv)
    out = lax.all_to_all(out, ("xh", "z0"), 0, 0, tiled=True)
    part = call(
        project_kernel,
        jax.ShapeDtypeStruct((2, 8, TQ, W), BF),
        [SMEM()] + [VMEM()] * 2,
        HBM(),
        "project",
        [pltpu.VMEM((2 * TQ, W), BF), pltpu.VMEM((2, 8, TQ, W), BF), pltpu.SemaphoreType.DMA((8,))],
    )((z0 & 1)[None], out, proj_weight)
    part = lax.all_to_all(part.reshape(16, TQ, W), ("g", "y", "c"), 0, 0, tiled=True)
    index = step_index[0]
    u_now = 1.0 - index.astype(F32) / STEPS
    u_next = 1.0 - (index + 1).astype(F32) / STEPS
    step = 3.0 * u_next / (1.0 + 2.0 * u_next) - 3.0 * u_now / (1.0 + 2.0 * u_now)
    shape = jax.ShapeDtypeStruct((1, TQ, W), BF)
    return call(finish_kernel, (shape, shape), [SMEM()] * 2 + [VMEM()] * 6, (VMEM(),) * 2, "finish")(
        guide[None],
        jnp.stack([guidance[guide], step]),
        part,
        img_hidden[0],
        gate[0],
        side,
        proj_bias[None],
        latent,
    )


def solution(mesh):
    fine = Mesh(mesh.devices.reshape(2, 2, NZ, NZ, 4, 2), ("g", "xh", "z1", "z0", "y", "c"))
    seq = ("xh", "z1", "z0")
    blk = ("y", "c")
    act = P("g", None, seq, blk)
    return jax.shard_map(
        shards,
        mesh=fine,
        in_specs=(
            act,
            act,
            act,
            act,
            act,
            act,
            P(),
            P(),
            P("g", None, blk),
            P(blk, None),
            P(blk),
            P(),
            P(),
            P(),
            P("g", seq, blk),
        ),
        out_specs=(P("g", seq, blk), P("g", seq, blk)),
        check_vma=False,
    )
```

```python
import functools

import jax
import jax.numpy as jnp
import numpy as np
from jax import lax
from jax.experimental import pallas as pl
from jax.experimental.pallas import tpu as pltpu
from jax.sharding import Mesh, PartitionSpec as P

HD = 128
GRID = 64
STEPS = 8
HPD = 3
W = HPD * HD
TQ = 64
TT = 16
TK = TQ + TT
NZ = 4
NS = 8
STAT = 8
BF = jnp.bfloat16
F32 = jnp.float32
VMEM_LIMIT = 48 * 1024 * 1024


def rope_tables():
    first = HD // 8
    second = (HD - first) // 2
    freqs = 10000.0 ** (-np.arange(0, second, 2).astype(np.float64) / second)
    n = freqs.shape[0]
    lane = np.arange(HD)
    pair = lane // 2
    sign = np.where(lane % 2 == 0, -1.0, 1.0)
    row_f = np.where((pair >= first // 2) & (pair < first // 2 + n), freqs[np.clip(pair - first // 2, 0, n - 1)], 0.0)
    col_f = np.where(pair >= first // 2 + n, freqs[np.clip(pair - first // 2 - n, 0, n - 1)], 0.0)
    rows = np.arange(32)[:, None] * row_f[None]
    cols = np.arange(GRID)[:, None] * col_f[None]
    return (
        np.stack([np.cos(rows), np.sin(rows) * sign]).astype(np.float32),
        np.stack([np.cos(cols), np.sin(cols) * sign]).astype(np.float32),
    )


def split3(x):
    hi = x.astype(BF)
    rest = x - hi.astype(F32)
    mid = rest.astype(BF)
    lo = (rest - mid.astype(F32)).astype(BF)
    return hi, mid, lo


def rope_of(row_ref, col_ref):
    in_row = lax.broadcasted_iota(jnp.int32, (TQ, HD), 1) < 72
    return jnp.where(in_row, row_ref[0], col_ref[0]), jnp.where(in_row, row_ref[1], col_ref[1])


def normed(x, gain):
    x = x.astype(F32)
    return x * lax.rsqrt(jnp.mean(x * x, -1, keepdims=True) + 1e-06) * gain


def rotated(x, table):
    even = lax.broadcasted_iota(jnp.int32, (TQ, HD), 1) % 2 == 0
    swapped = jnp.where(even, pltpu.roll(x, HD - 1, 1), pltpu.roll(x, 1, 1))
    return x * table[0] + swapped * table[1]


def start_all(pairs, sems):
    copies = [pltpu.make_async_copy(src, dst, sems.at[i]) for i, (src, dst) in enumerate(pairs)]
    for copy in copies:
        copy.start()
    return copies


def keys_kernel(
    seq_id, xh_id, k_hbm, v_hbm, tk_hbm, tv_hbm, kg_hbm, row_hbm, col_hbm, after_hbm,
    keep_out, send_out,
    k_ref, v_ref, tk_ref, tv_ref, kg_ref, row_ref, col_ref, sems,
):
    rows = row_hbm.at[:, pl.ds(seq_id[0], 1)]
    copies = start_all(
        ((rows, row_ref), (col_hbm, col_ref), (kg_hbm, kg_ref), (tk_hbm, tk_ref), (k_hbm, k_ref), (v_hbm, v_ref), (tv_hbm, tv_ref)),
        sems,
    )
    for copy in copies[:5]:
        copy.wait()
    table = rope_of(row_ref, col_ref)
    own = xh_id[0]
    for out, p in ((send_out, 1 - own), (keep_out, own)):
        for h in range(HPD):
            hs = slice(h * HD, (h + 1) * HD)
            out[0, 0:TT, hs] = normed(tk_ref[p, :, hs], kg_ref[1:2]).astype(BF)
            out[0, TT:TK, hs] = rotated(normed(k_ref[p, :, hs], kg_ref[0:1]), table).astype(BF)
    for copy in copies[5:]:
        copy.wait()
    for out, p in ((send_out, 1 - own), (keep_out, own)):
        out[1, 0:TT, :] = tv_ref[p]
        out[1, TT:TK, :] = v_ref[p]


def queries_kernel(
    seq_id, guide_id, q_hbm, hid_hbm, gate_hbm, qg_hbm, row_hbm, col_hbm,
    q_out, side_out,
    q_ref, hid_ref, gate_ref, qg_ref, row_ref, col_ref, sems,
):
    other = 1 - guide_id[0]
    rows = row_hbm.at[:, pl.ds(seq_id[0], 1)]
    copies = start_all(
        ((rows, row_ref), (col_hbm, col_ref), (qg_hbm, qg_ref), (q_hbm, q_ref), (hid_hbm.at[other], hid_ref), (gate_hbm, gate_ref)),
        sems,
    )
    for copy in copies[:4]:
        copy.wait()
    table = rope_of(row_ref, col_ref)
    for p in range(2):
        for h in range(HPD):
            hs = slice(h * HD, (h + 1) * HD)
            q = rotated(normed(q_ref[p, :, hs], qg_ref[...]), table).astype(BF)
            for z in range(NZ):
                q_out[p * NZ + z, :, hs] = q
    for copy in copies[4:]:
        copy.wait()
    side_out[0:TQ, :] = hid_ref[...]
    hi, mid, lo = split3(gate_ref[pl.ds(other, 1), :])
    rows = lax.broadcasted_iota(jnp.int32, (8, W), 0)
    packed = jnp.where(rows == 0, hi.astype(F32), jnp.where(rows == 1, mid.astype(F32), lo.astype(F32)))
    side_out[TQ : TQ + 8, :] = packed.astype(BF)


def attend_kernel(xh_id, z0_id, len_ref, q_ref, kv_ref, out_ref):
    scale = HD ** (-0.5) * 1.4426950408889634
    own = xh_id[0]
    at = lax.broadcasted_iota(jnp.int32, (1, NS * TK), 1)
    block = jnp.zeros_like(at)
    for i in range(1, NS):
        block = block + (at >= i * TK).astype(jnp.int32)
    within = at - block * TK
    from_own = (block & 1) == 0
    seq = (jnp.where(from_own, own, 1 - own) * NZ + (block >> 1)) * NZ + z0_id[0]
    dead = (within < TT) & (seq * TT + within >= len_ref[own])
    bias = jnp.where(dead, -1e30, 0.0)
    lane = lax.broadcasted_iota(jnp.int32, (NS * TQ, HD), 1)
    stats = jnp.zeros((NS * TQ, HD), F32)
    for h in range(HPD):
        hs = slice(h * HD, (h + 1) * HD)
        q = q_ref[:, :, hs].reshape(NS * TQ, HD)
        k = kv_ref[:, :, 0, :, hs].reshape(NS * TK, HD)
        v = kv_ref[:, :, 1, :, hs].reshape(NS * TK, HD)
        s = lax.dot_general(q, k, (((1,), (1,)), ((), ())), preferred_element_type=F32)
        s = s * scale + bias
        top = jnp.max(s, -1, keepdims=True)
        e = jnp.exp2(s - top)
        total = jnp.sum(e, -1, keepdims=True)
        o = jnp.dot(e.astype(BF), v, preferred_element_type=F32) / total
        out_ref[:, 0:TQ, hs] = o.astype(BF).reshape(NS, TQ, HD)
        lse = top + jnp.log2(total)
        hi = lse.astype(BF).astype(F32)
        stats = jnp.where(lane == h, hi, jnp.where(lane == HPD + h, lse - hi, stats))
    rows = jnp.transpose(stats)[0:STAT, :].astype(BF)
    for d in range(NS):
        a = (d // 2) * HD
        out_ref[d, TQ : TQ + STAT, 0:HD] = rows[:, a : a + HD]
        out_ref[d, TQ : TQ + STAT, HD:W] = jnp.zeros((STAT, W - HD), BF)


def project_kernel(ids, o_ref, w_ref, out_hbm, attn_ref, out_ref, sems):
    odd = ids[0]
    stats = o_ref[:, TQ : TQ + STAT, 0:HD].astype(F32).reshape(NS * STAT, HD)
    cols = jnp.transpose(jnp.concatenate([stats, stats], 0))
    cols = jnp.where(odd == 0, cols[0:TQ], cols[TQ : 2 * TQ])
    for p in range(2):
        for h in range(HPD):
            hs = slice(h * HD, (h + 1) * HD)
            lses = []
            for z in range(NZ):
                at = (p * NZ + z) * STAT + h
                lses.append(cols[:, at : at + 1] + cols[:, at + HPD : at + HPD + 1])
            top = functools.reduce(jnp.maximum, lses)
            ws = [jnp.exp2(x - top) for x in lses]
            total = functools.reduce(jnp.add, ws)
            acc = jnp.zeros((TQ, HD), F32)
            for z in range(NZ):
                acc = acc + ws[z] * o_ref[p * NZ + z, 0:TQ, hs].astype(F32)
            attn_ref[p * TQ : (p + 1) * TQ, hs] = (acc / total).astype(BF)
    attn = attn_ref[...]
    copies = []
    for b in range(8):
        part = jnp.dot(attn, w_ref[:, b * W : (b + 1) * W], preferred_element_type=F32).astype(BF)
        out_ref[0, b] = part[0:TQ]
        out_ref[1, b] = part[TQ : 2 * TQ]
        copy = pltpu.make_async_copy(out_ref.at[:, b], out_hbm.at[:, b], sems.at[b])
        copy.start()
        copies.append(copy)
    for copy in copies:
        copy.wait()


def finish_kernel(ids, scal, part_ref, hid_ref, gate_ref, side_ref, bias_ref, lat_ref, guided_ref, next_ref):
    mine = ids[0]
    mine_f = mine.astype(F32)
    outs = []
    other_gate = (
        side_ref[TQ : TQ + 1, :].astype(F32) + side_ref[TQ + 1 : TQ + 2, :].astype(F32)
    ) + side_ref[TQ + 2 : TQ + 3, :].astype(F32)
    for g in range(2):
        acc = part_ref[g * 8].astype(F32)
        for b in range(1, 8):
            acc = acc + part_ref[g * 8 + b].astype(F32)
        own = mine == g
        hidden = jnp.where(own, hid_ref[mine].astype(F32), side_ref[0:TQ, :].astype(F32))
        gate = jnp.where(own, gate_ref[pl.ds(mine, 1), :], other_gate)
        outs.append((hidden + gate * (acc + bias_ref[...])).astype(BF).astype(F32))
    cond, uncond = outs
    guided = uncond + scal[0] * (cond - uncond)
    guided_ref[0] = guided.astype(BF)
    next_ref[0] = (lat_ref[0].astype(F32) + scal[1] * guided).astype(BF)


SMEM = functools.partial(pl.BlockSpec, memory_space=pltpu.SMEM)
VMEM = functools.partial(pl.BlockSpec, memory_space=pltpu.VMEM)
HBM = functools.partial(pl.BlockSpec, memory_space=pltpu.HBM)


def call(kernel, outs, ins, out_specs, name, scratch=(), limit=VMEM_LIMIT):
    return pl.pallas_call(
        kernel,
        out_shape=outs,
        in_specs=ins,
        out_specs=out_specs,
        scratch_shapes=list(scratch),
        compiler_params=pltpu.CompilerParams(vmem_limit_bytes=limit),
        name=name,
    )


def shards(
    img_hidden,
    img_query,
    img_key,
    img_value,
    txt_key,
    txt_value,
    query_gain,
    key_gain,
    gate,
    proj_weight,
    proj_bias,
    guidance,
    text_len,
    step_index,
    latent,
):
    guide = lax.axis_index("g")
    xh = lax.axis_index("xh")
    z1 = lax.axis_index("z1")
    z0 = lax.axis_index("z0")
    seq = (xh * NZ + z1) * NZ + z0
    rows, cols = rope_tables()
    kv_shape = jax.ShapeDtypeStruct((2, TK, W), BF)
    row_t = jnp.asarray(rows)
    col_t = jnp.asarray(cols)
    rope_scratch = [pltpu.VMEM((2, 1, HD), F32), pltpu.VMEM((2, TQ, HD), F32)]
    q, side = call(
        queries_kernel,
        (jax.ShapeDtypeStruct((NS, TQ, W), BF), jax.ShapeDtypeStruct((TQ + 8, W), BF)),
        [SMEM()] * 2 + [HBM()] * 6,
        (VMEM(),) * 2,
        "queries",
        [
            pltpu.VMEM((2, TQ, W), BF),
            pltpu.VMEM((TQ, W), BF),
            pltpu.VMEM((2, W), F32),
            pltpu.VMEM((1, HD), F32),
            *rope_scratch,
            pltpu.SemaphoreType.DMA((6,)),
        ],
        63 * 1024 * 1024,
    )(seq[None], guide[None], img_query[0], img_hidden[0], gate[0], query_gain[None], row_t, col_t)
    keep, send = call(
        keys_kernel,
        (kv_shape, kv_shape),
        [SMEM()] * 2 + [HBM()] * 8,
        (VMEM(),) * 2,
        "keys",
        [
            pltpu.VMEM((2, TQ, W), BF),
            pltpu.VMEM((2, TQ, W), BF),
            pltpu.VMEM((2, TT, W), BF),
            pltpu.VMEM((2, TT, W), BF),
            pltpu.VMEM((2, HD), F32),
            *rope_scratch,
            pltpu.SemaphoreType.DMA((7,)),
        ],
        63 * 1024 * 1024,
    )(seq[None], xh[None], img_key[0], img_value[0], txt_key[0], txt_value[0], key_gain, row_t, col_t, q)
    q = lax.all_to_all(q, ("xh", "z0"), 0, 0, tiled=True)
    swap = [(0, 1), (1, 0)]
    got = lax.ppermute(send, "xh", swap)
    side = lax.ppermute(side, "g", swap)
    got, side = lax.optimization_barrier((got, side))
    kv = lax.all_gather(jnp.stack([keep, got]), "z1", axis=0)

    out = call(
        attend_kernel,
        jax.ShapeDtypeStruct((NS, TQ + STAT, W), BF),
        [SMEM()] * 3 + [VMEM()] * 2,
        VMEM(),
        "attend",
    )(xh[None], z0[None], text_len, q, kv)
    out = lax.all_to_all(out, ("xh", "z0"), 0, 0, tiled=True)
    part = call(
        project_kernel,
        jax.ShapeDtypeStruct((2, 8, TQ, W), BF),
        [SMEM()] + [VMEM()] * 2,
        HBM(),
        "project",
        [pltpu.VMEM((2 * TQ, W), BF), pltpu.VMEM((2, 8, TQ, W), BF), pltpu.SemaphoreType.DMA((8,))],
    )((z0 & 1)[None], out, proj_weight)
    part = lax.all_to_all(part.reshape(16, TQ, W), ("g", "y", "c"), 0, 0, tiled=True)
    index = step_index[0]
    u_now = 1.0 - index.astype(F32) / STEPS
    u_next = 1.0 - (index + 1).astype(F32) / STEPS
    step = 3.0 * u_next / (1.0 + 2.0 * u_next) - 3.0 * u_now / (1.0 + 2.0 * u_now)
    shape = jax.ShapeDtypeStruct((1, TQ, W), BF)
    return call(finish_kernel, (shape, shape), [SMEM()] * 2 + [VMEM()] * 6, (VMEM(),) * 2, "finish")(
        guide[None],
        jnp.stack([guidance[guide], step]),
        part,
        img_hidden[0],
        gate[0],
        side,
        proj_bias[None],
        latent,
    )


def solution(mesh):
    fine = Mesh(mesh.devices.reshape(2, 2, NZ, NZ, 4, 2), ("g", "xh", "z1", "z0", "y", "c"))
    seq = ("xh", "z1", "z0")
    blk = ("y", "c")
    act = P("g", None, seq, blk)
    return jax.shard_map(
        shards,
        mesh=fine,
        in_specs=(
            act,
            act,
            act,
            act,
            act,
            act,
            P(),
            P(),
            P("g", None, blk),
            P(blk, None),
            P(blk),
            P(),
            P(),
            P(),
            P("g", seq, blk),
        ),
        out_specs=(P("g", seq, blk), P("g", seq, blk)),
        check_vma=False,
    )
```

```python
import functools

import jax
import jax.numpy as jnp
import numpy as np
from jax import lax
from jax.experimental import pallas as pl
from jax.experimental.pallas import tpu as pltpu
from jax.sharding import Mesh, PartitionSpec as P

HD = 128
GRID = 64
STEPS = 8
HPD = 3
W = HPD * HD
TQ = 64
TT = 16
TK = TQ + TT
NZ = 4
NS = 8
STAT = 8
BF = jnp.bfloat16
F32 = jnp.float32
VMEM_LIMIT = 48 * 1024 * 1024


def rope_tables():
    first = HD // 8
    second = (HD - first) // 2
    freqs = 10000.0 ** (-np.arange(0, second, 2).astype(np.float64) / second)
    n = freqs.shape[0]
    lane = np.arange(HD)
    pair = lane // 2
    sign = np.where(lane % 2 == 0, -1.0, 1.0)
    row_f = np.where((pair >= first // 2) & (pair < first // 2 + n), freqs[np.clip(pair - first // 2, 0, n - 1)], 0.0)
    col_f = np.where(pair >= first // 2 + n, freqs[np.clip(pair - first // 2 - n, 0, n - 1)], 0.0)
    rows = np.arange(32)[:, None] * row_f[None]
    cols = np.arange(GRID)[:, None] * col_f[None]
    return (
        np.stack([np.cos(rows), np.sin(rows) * sign]).astype(np.float32),
        np.stack([np.cos(cols), np.sin(cols) * sign]).astype(np.float32),
    )


def split3(x):
    hi = x.astype(BF)
    rest = x - hi.astype(F32)
    mid = rest.astype(BF)
    lo = (rest - mid.astype(F32)).astype(BF)
    return hi, mid, lo


def rope_of(row_ref, col_ref):
    in_row = lax.broadcasted_iota(jnp.int32, (TQ, HD), 1) < 72
    return jnp.where(in_row, row_ref[0], col_ref[0]), jnp.where(in_row, row_ref[1], col_ref[1])


def normed(x, gain):
    x = x.astype(F32)
    return x * lax.rsqrt(jnp.mean(x * x, -1, keepdims=True) + 1e-06) * gain


def rotated(x, table):
    even = lax.broadcasted_iota(jnp.int32, (TQ, HD), 1) % 2 == 0
    swapped = jnp.where(even, pltpu.roll(x, HD - 1, 1), pltpu.roll(x, 1, 1))
    return x * table[0] + swapped * table[1]


def start_all(pairs, sems):
    copies = [pltpu.make_async_copy(src, dst, sems.at[i]) for i, (src, dst) in enumerate(pairs)]
    for copy in copies:
        copy.start()
    return copies


def prepare_kernel(
    seq_id, xh_id, guide_id, k_hbm, q_hbm, v_hbm, tk_hbm, tv_hbm, hid_hbm, gate_hbm, qg_hbm, kg_hbm, row_hbm, col_hbm,
    keep_out, send_out, q_out, side_out,
    k_ref, q_ref, v_ref, tk_ref, tv_ref, hid_ref, gate_ref, qg_ref, kg_ref, row_ref, col_ref, sems,
):
    other = 1 - guide_id[0]
    rows = row_hbm.at[:, pl.ds(seq_id[0], 1)]
    copies = start_all(
        (
            (rows, row_ref), (col_hbm, col_ref), (qg_hbm, qg_ref), (q_hbm, q_ref), (kg_hbm, kg_ref), (tk_hbm, tk_ref), (k_hbm, k_ref),
            (v_hbm, v_ref), (tv_hbm, tv_ref), (hid_hbm.at[other], hid_ref), (gate_hbm, gate_ref),
        ),
        sems,
    )
    for copy in copies[:4]:
        copy.wait()
    table = rope_of(row_ref, col_ref)
    for p in range(2):
        for h in range(HPD):
            hs = slice(h * HD, (h + 1) * HD)
            q = rotated(normed(q_ref[p, :, hs], qg_ref[...]), table).astype(BF)
            for z in range(NZ):
                q_out[p * NZ + z, :, hs] = q
    for copy in copies[4:7]:
        copy.wait()
    own = xh_id[0]
    for out, p in ((keep_out, own), (send_out, 1 - own)):
        for h in range(HPD):
            hs = slice(h * HD, (h + 1) * HD)
            out[0, 0:TT, hs] = normed(tk_ref[p, :, hs], kg_ref[1:2]).astype(BF)
            out[0, TT:TK, hs] = rotated(normed(k_ref[p, :, hs], kg_ref[0:1]), table).astype(BF)
    for copy in copies[7:]:
        copy.wait()
    for out, p in ((keep_out, own), (send_out, 1 - own)):
        out[1, 0:TT, :] = tv_ref[p]
        out[1, TT:TK, :] = v_ref[p]
    side_out[0:TQ, :] = hid_ref[...]
    hi, mid, lo = split3(gate_ref[pl.ds(other, 1), :])
    rows = lax.broadcasted_iota(jnp.int32, (8, W), 0)
    packed = jnp.where(rows == 0, hi.astype(F32), jnp.where(rows == 1, mid.astype(F32), lo.astype(F32)))
    side_out[TQ : TQ + 8, :] = packed.astype(BF)


def attend_kernel(xh_id, z0_id, len_ref, q_hbm, kv_hbm, out_hbm, q_ref, kv_ref, out_ref, in_sems, out_sems):
    loads = []
    for h in range(HPD):
        hs = slice(h * HD, (h + 1) * HD)
        loads.append(
            start_all(
                (
                    (q_hbm.at[:, :, hs], q_ref.at[:, :, hs]),
                    (kv_hbm.at[:, :, 0, :, hs], kv_ref.at[:, :, 0, :, hs]),
                    (kv_hbm.at[:, :, 1, :, hs], kv_ref.at[:, :, 1, :, hs]),
                ),
                in_sems.at[h],
            )
        )
    stores = []
    scale = HD ** (-0.5) * 1.4426950408889634
    own = xh_id[0]
    at = lax.broadcasted_iota(jnp.int32, (1, NS * TK), 1)
    block = jnp.zeros_like(at)
    for i in range(1, NS):
        block = block + (at >= i * TK).astype(jnp.int32)
    within = at - block * TK
    from_own = (block & 1) == 0
    seq = (jnp.where(from_own, own, 1 - own) * NZ + (block >> 1)) * NZ + z0_id[0]
    dead = (within < TT) & (seq * TT + within >= len_ref[own])
    bias = jnp.where(dead, -1e30, 0.0)
    lane = lax.broadcasted_iota(jnp.int32, (NS * TQ, HD), 1)
    stats = jnp.zeros((NS * TQ, HD), F32)
    for h in range(HPD):
        hs = slice(h * HD, (h + 1) * HD)
        loads[h][0].wait()
        loads[h][1].wait()
        q = q_ref[:, :, hs].reshape(NS * TQ, HD)
        k = kv_ref[:, :, 0, :, hs].reshape(NS * TK, HD)
        s = lax.dot_general(q, k, (((1,), (1,)), ((), ())), preferred_element_type=F32)
        s = s * scale + bias
        top = jnp.max(s, -1, keepdims=True)
        e = jnp.exp2(s - top)
        total = jnp.sum(e, -1, keepdims=True)
        loads[h][2].wait()
        v = kv_ref[:, :, 1, :, hs].reshape(NS * TK, HD)
        o = jnp.dot(e.astype(BF), v, preferred_element_type=F32) / total
        out_ref[:, 0:TQ, hs] = o.astype(BF).reshape(NS, TQ, HD)
        stores += start_all(((out_ref.at[:, 0:TQ, hs], out_hbm.at[:, 0:TQ, hs]),), out_sems.at[pl.ds(h, 1)])
        lse = top + jnp.log2(total)
        hi = lse.astype(BF).astype(F32)
        stats = jnp.where(lane == h, hi, jnp.where(lane == HPD + h, lse - hi, stats))
    rows = jnp.transpose(stats)[0:STAT, :].astype(BF)
    for d in range(NS):
        a = (d // 2) * HD
        out_ref[d, TQ : TQ + STAT, 0:HD] = rows[:, a : a + HD]
        out_ref[d, TQ : TQ + STAT, HD:W] = jnp.zeros((STAT, W - HD), BF)
    tail = slice(TQ, TQ + STAT)
    stores += start_all(((out_ref.at[:, tail], out_hbm.at[:, tail]),), out_sems.at[pl.ds(HPD, 1)])
    for copy in stores:
        copy.wait()


def project_kernel(ids, o_ref, w_ref, out_hbm, attn_ref, out_ref, sems):
    odd = ids[0]
    stats = o_ref[:, TQ : TQ + STAT, 0:HD].astype(F32).reshape(NS * STAT, HD)
    cols = jnp.transpose(jnp.concatenate([stats, stats], 0))
    cols = jnp.where(odd == 0, cols[0:TQ], cols[TQ : 2 * TQ])
    for p in range(2):
        for h in range(HPD):
            hs = slice(h * HD, (h + 1) * HD)
            lses = []
            for z in range(NZ):
                at = (p * NZ + z) * STAT + h
                lses.append(cols[:, at : at + 1] + cols[:, at + HPD : at + HPD + 1])
            top = functools.reduce(jnp.maximum, lses)
            ws = [jnp.exp2(x - top) for x in lses]
            total = functools.reduce(jnp.add, ws)
            acc = jnp.zeros((TQ, HD), F32)
            for z in range(NZ):
                acc = acc + ws[z] * o_ref[p * NZ + z, 0:TQ, hs].astype(F32)
            attn_ref[p * TQ : (p + 1) * TQ, hs] = (acc / total).astype(BF)
    attn = attn_ref[...]
    copies = []
    for b in range(8):
        part = jnp.dot(attn, w_ref[:, b * W : (b + 1) * W], preferred_element_type=F32).astype(BF)
        out_ref[0, b] = part[0:TQ]
        out_ref[1, b] = part[TQ : 2 * TQ]
        copy = pltpu.make_async_copy(out_ref.at[:, b], out_hbm.at[:, b], sems.at[b])
        copy.start()
        copies.append(copy)
    for copy in copies:
        copy.wait()


def finish_kernel(ids, scal, part_ref, hid_ref, gate_ref, side_ref, bias_ref, lat_ref, guided_ref, next_ref):
    mine = ids[0]
    mine_f = mine.astype(F32)
    outs = []
    other_gate = (
        side_ref[TQ : TQ + 1, :].astype(F32) + side_ref[TQ + 1 : TQ + 2, :].astype(F32)
    ) + side_ref[TQ + 2 : TQ + 3, :].astype(F32)
    for g in range(2):
        acc = part_ref[g * 8].astype(F32)
        for b in range(1, 8):
            acc = acc + part_ref[g * 8 + b].astype(F32)
        own = mine == g
        hidden = jnp.where(own, hid_ref[mine].astype(F32), side_ref[0:TQ, :].astype(F32))
        gate = jnp.where(own, gate_ref[pl.ds(mine, 1), :], other_gate)
        outs.append((hidden + gate * (acc + bias_ref[...])).astype(BF).astype(F32))
    cond, uncond = outs
    guided = uncond + scal[0] * (cond - uncond)
    guided_ref[0] = guided.astype(BF)
    next_ref[0] = (lat_ref[0].astype(F32) + scal[1] * guided).astype(BF)


SMEM = functools.partial(pl.BlockSpec, memory_space=pltpu.SMEM)
VMEM = functools.partial(pl.BlockSpec, memory_space=pltpu.VMEM)
HBM = functools.partial(pl.BlockSpec, memory_space=pltpu.HBM)


def call(kernel, outs, ins, out_specs, name, scratch=(), limit=VMEM_LIMIT):
    return pl.pallas_call(
        kernel,
        out_shape=outs,
        in_specs=ins,
        out_specs=out_specs,
        scratch_shapes=list(scratch),
        compiler_params=pltpu.CompilerParams(vmem_limit_bytes=limit),
        name=name,
    )


def shards(
    img_hidden,
    img_query,
    img_key,
    img_value,
    txt_key,
    txt_value,
    query_gain,
    key_gain,
    gate,
    proj_weight,
    proj_bias,
    guidance,
    text_len,
    step_index,
    latent,
):
    guide = lax.axis_index("g")
    xh = lax.axis_index("xh")
    z1 = lax.axis_index("z1")
    z0 = lax.axis_index("z0")
    seq = (xh * NZ + z1) * NZ + z0
    rows, cols = rope_tables()
    kv_shape = jax.ShapeDtypeStruct((2, TK, W), BF)
    keep, send, q, side = call(
        prepare_kernel,
        (kv_shape, kv_shape, jax.ShapeDtypeStruct((NS, TQ, W), BF), jax.ShapeDtypeStruct((TQ + 8, W), BF)),
        [SMEM()] * 3 + [HBM()] * 11,
        (VMEM(),) * 4,
        "prepare",
        [
            pltpu.VMEM((2, TQ, W), BF),
            pltpu.VMEM((2, TQ, W), BF),
            pltpu.VMEM((2, TQ, W), BF),
            pltpu.VMEM((2, TT, W), BF),
            pltpu.VMEM((2, TT, W), BF),
            pltpu.VMEM((TQ, W), BF),
            pltpu.VMEM((2, W), F32),
            pltpu.VMEM((1, HD), F32),
            pltpu.VMEM((2, HD), F32),
            pltpu.VMEM((2, 1, HD), F32),
            pltpu.VMEM((2, TQ, HD), F32),
            pltpu.SemaphoreType.DMA((11,)),
        ],
        63 * 1024 * 1024,
    )(
        seq[None],
        xh[None],
        guide[None],
        img_key[0],
        img_query[0],
        img_value[0],
        txt_key[0],
        txt_value[0],
        img_hidden[0],
        gate[0],
        query_gain[None],
        key_gain,
        jnp.asarray(rows),
        jnp.asarray(cols),
    )
    q = lax.all_to_all(q, ("xh", "z0"), 0, 0, tiled=True)
    swap = [(0, 1), (1, 0)]
    got = lax.ppermute(send, "xh", swap)
    kv = lax.all_gather(jnp.stack([keep, got]), "z1", axis=0)

    out = call(
        attend_kernel,
        jax.ShapeDtypeStruct((NS, TQ + STAT, W), BF),
        [SMEM()] * 3 + [HBM()] * 2,
        HBM(),
        "attend",
        [
            pltpu.VMEM((NS, TQ, W), BF),
            pltpu.VMEM((NZ, 2, 2, TK, W), BF),
            pltpu.VMEM((NS, TQ + STAT, W), BF),
            pltpu.SemaphoreType.DMA((HPD, 3)),
            pltpu.SemaphoreType.DMA((HPD + 1,)),
        ],
        63 * 1024 * 1024,
    )(xh[None], z0[None], text_len, q, kv)
    out, side = lax.optimization_barrier((out, side))
    side = lax.ppermute(side, "g", swap)
    out = lax.all_to_all(out, ("xh", "z0"), 0, 0, tiled=True)
    out, side = lax.optimization_barrier((out, side))
    part = call(
        project_kernel,
        jax.ShapeDtypeStruct((2, 8, TQ, W), BF),
        [SMEM()] + [VMEM()] * 2,
        HBM(),
        "project",
        [pltpu.VMEM((2 * TQ, W), BF), pltpu.VMEM((2, 8, TQ, W), BF), pltpu.SemaphoreType.DMA((8,))],
    )((z0 & 1)[None], out, proj_weight)
    part = lax.all_to_all(part.reshape(16, TQ, W), ("g", "y", "c"), 0, 0, tiled=True)
    index = step_index[0]
    u_now = 1.0 - index.astype(F32) / STEPS
    u_next = 1.0 - (index + 1).astype(F32) / STEPS
    step = 3.0 * u_next / (1.0 + 2.0 * u_next) - 3.0 * u_now / (1.0 + 2.0 * u_now)
    shape = jax.ShapeDtypeStruct((1, TQ, W), BF)
    return call(finish_kernel, (shape, shape), [SMEM()] * 2 + [VMEM()] * 6, (VMEM(),) * 2, "finish")(
        guide[None],
        jnp.stack([guidance[guide], step]),
        part,
        img_hidden[0],
        gate[0],
        side,
        proj_bias[None],
        latent,
    )


def solution(mesh):
    fine = Mesh(mesh.devices.reshape(2, 2, NZ, NZ, 4, 2), ("g", "xh", "z1", "z0", "y", "c"))
    seq = ("xh", "z1", "z0")
    blk = ("y", "c")
    act = P("g", None, seq, blk)
    return jax.shard_map(
        shards,
        mesh=fine,
        in_specs=(
            act,
            act,
            act,
            act,
            act,
            act,
            P(),
            P(),
            P("g", None, blk),
            P(blk, None),
            P(blk),
            P(),
            P(),
            P(),
            P("g", seq, blk),
        ),
        out_specs=(P("g", seq, blk), P("g", seq, blk)),
        check_vma=False,
    )
```

```python
import functools

import jax
import jax.numpy as jnp
import numpy as np
from jax import lax
from jax.experimental import pallas as pl
from jax.experimental.pallas import tpu as pltpu
from jax.sharding import Mesh, PartitionSpec as P

HD = 128
GRID = 64
STEPS = 8
HPD = 3
W = HPD * HD
TQ = 64
TT = 16
TK = TQ + TT
NZ = 4
NS = 8
STAT = 8
BF = jnp.bfloat16
F32 = jnp.float32
VMEM_LIMIT = 48 * 1024 * 1024


def rope_tables():
    first = HD // 8
    second = (HD - first) // 2
    freqs = 10000.0 ** (-np.arange(0, second, 2).astype(np.float64) / second)
    n = freqs.shape[0]
    lane = np.arange(HD)
    pair = lane // 2
    sign = np.where(lane % 2 == 0, -1.0, 1.0)
    row_f = np.where((pair >= first // 2) & (pair < first // 2 + n), freqs[np.clip(pair - first // 2, 0, n - 1)], 0.0)
    col_f = np.where(pair >= first // 2 + n, freqs[np.clip(pair - first // 2 - n, 0, n - 1)], 0.0)
    rows = np.arange(32)[:, None] * row_f[None]
    cols = np.arange(GRID)[:, None] * col_f[None]
    return (
        np.stack([np.cos(rows), np.sin(rows) * sign]).astype(np.float32),
        np.stack([np.cos(cols), np.sin(cols) * sign]).astype(np.float32),
    )


def split3(x):
    hi = x.astype(BF)
    rest = x - hi.astype(F32)
    mid = rest.astype(BF)
    lo = (rest - mid.astype(F32)).astype(BF)
    return hi, mid, lo


def rope_of(row_ref, col_ref):
    in_row = lax.broadcasted_iota(jnp.int32, (TQ, HD), 1) < 72
    return jnp.where(in_row, row_ref[0], col_ref[0]), jnp.where(in_row, row_ref[1], col_ref[1])


def normed(x, gain):
    x = x.astype(F32)
    return x * lax.rsqrt(jnp.mean(x * x, -1, keepdims=True) + 1e-06) * gain


def rotated(x, table):
    even = lax.broadcasted_iota(jnp.int32, (TQ, HD), 1) % 2 == 0
    swapped = jnp.where(even, pltpu.roll(x, HD - 1, 1), pltpu.roll(x, 1, 1))
    return x * table[0] + swapped * table[1]


def start_all(pairs, sems):
    copies = [pltpu.make_async_copy(src, dst, sems.at[i]) for i, (src, dst) in enumerate(pairs)]
    for copy in copies:
        copy.start()
    return copies


def prepare_kernel(
    seq_id, xh_id, guide_id, k_hbm, q_hbm, v_hbm, tk_hbm, tv_hbm, hid_hbm, gate_hbm, qg_hbm, kg_hbm, row_hbm, col_hbm,
    keep_out, send_out, q_out, side_out,
    k_ref, q_ref, v_ref, tk_ref, tv_ref, hid_ref, gate_ref, qg_ref, kg_ref, row_ref, col_ref, sems,
):
    other = 1 - guide_id[0]
    rows = row_hbm.at[:, pl.ds(seq_id[0], 1)]
    copies = start_all(
        (
            (rows, row_ref), (col_hbm, col_ref), (qg_hbm, qg_ref), (q_hbm, q_ref), (kg_hbm, kg_ref), (tk_hbm, tk_ref), (k_hbm, k_ref),
            (v_hbm, v_ref), (tv_hbm, tv_ref), (hid_hbm.at[other], hid_ref), (gate_hbm, gate_ref),
        ),
        sems,
    )
    for copy in copies[:4]:
        copy.wait()
    table = rope_of(row_ref, col_ref)
    for p in range(2):
        for h in range(HPD):
            hs = slice(h * HD, (h + 1) * HD)
            q = rotated(normed(q_ref[p, :, hs], qg_ref[...]), table).astype(BF)
            for z in range(NZ):
                q_out[p * NZ + z, :, hs] = q
    for copy in copies[4:7]:
        copy.wait()
    own = xh_id[0]
    for out, p in ((keep_out, own), (send_out, 1 - own)):
        for h in range(HPD):
            hs = slice(h * HD, (h + 1) * HD)
            out[0, 0:TT, hs] = normed(tk_ref[p, :, hs], kg_ref[1:2]).astype(BF)
            out[0, TT:TK, hs] = rotated(normed(k_ref[p, :, hs], kg_ref[0:1]), table).astype(BF)
    for copy in copies[7:]:
        copy.wait()
    for out, p in ((keep_out, own), (send_out, 1 - own)):
        out[1, 0:TT, :] = tv_ref[p]
        out[1, TT:TK, :] = v_ref[p]
    side_out[0:TQ, :] = hid_ref[...]
    hi, mid, lo = split3(gate_ref[pl.ds(other, 1), :])
    rows = lax.broadcasted_iota(jnp.int32, (8, W), 0)
    packed = jnp.where(rows == 0, hi.astype(F32), jnp.where(rows == 1, mid.astype(F32), lo.astype(F32)))
    side_out[TQ : TQ + 8, :] = packed.astype(BF)


def join_kernel(keep_ref, got_ref, out_ref):
    out_ref[0] = keep_ref[...]
    out_ref[1] = got_ref[...]


def attend_kernel(xh_id, z0_id, len_ref, q_ref, kv_ref, out_ref):
    scale = HD ** (-0.5) * 1.4426950408889634
    own = xh_id[0]
    at = lax.broadcasted_iota(jnp.int32, (1, NS * TK), 1)
    block = jnp.zeros_like(at)
    for i in range(1, NS):
        block = block + (at >= i * TK).astype(jnp.int32)
    within = at - block * TK
    from_own = (block & 1) == 0
    seq = (jnp.where(from_own, own, 1 - own) * NZ + (block >> 1)) * NZ + z0_id[0]
    dead = (within < TT) & (seq * TT + within >= len_ref[own])
    bias = jnp.where(dead, -1e30, 0.0)
    lane = lax.broadcasted_iota(jnp.int32, (NS * TQ, HD), 1)
    stats = jnp.zeros((NS * TQ, HD), F32)
    for h in range(HPD):
        hs = slice(h * HD, (h + 1) * HD)
        q = q_ref[:, :, hs].reshape(NS * TQ, HD)
        k = kv_ref[:, :, 0, :, hs].reshape(NS * TK, HD)
        v = kv_ref[:, :, 1, :, hs].reshape(NS * TK, HD)
        s = lax.dot_general(q, k, (((1,), (1,)), ((), ())), preferred_element_type=F32)
        s = s * scale + bias
        top = jnp.max(s, -1, keepdims=True)
        e = jnp.exp2(s - top)
        total = jnp.sum(e, -1, keepdims=True)
        o = jnp.dot(e.astype(BF), v, preferred_element_type=F32) / total
        out_ref[:, 0:TQ, hs] = o.astype(BF).reshape(NS, TQ, HD)
        lse = top + jnp.log2(total)
        hi = lse.astype(BF).astype(F32)
        stats = jnp.where(lane == h, hi, jnp.where(lane == HPD + h, lse - hi, stats))
    rows = jnp.transpose(stats)[0:STAT, :].astype(BF)
    for d in range(NS):
        a = (d // 2) * HD
        out_ref[d, TQ : TQ + STAT, 0:HD] = rows[:, a : a + HD]
        out_ref[d, TQ : TQ + STAT, HD:W] = jnp.zeros((STAT, W - HD), BF)


def project_kernel(ids, o_ref, w_ref, out_hbm, attn_ref, out_ref, sems):
    odd = ids[0]
    stats = o_ref[:, TQ : TQ + STAT, 0:HD].astype(F32).reshape(NS * STAT, HD)
    cols = jnp.transpose(jnp.concatenate([stats, stats], 0))
    cols = jnp.where(odd == 0, cols[0:TQ], cols[TQ : 2 * TQ])
    for p in range(2):
        for h in range(HPD):
            hs = slice(h * HD, (h + 1) * HD)
            lses = []
            for z in range(NZ):
                at = (p * NZ + z) * STAT + h
                lses.append(cols[:, at : at + 1] + cols[:, at + HPD : at + HPD + 1])
            top = functools.reduce(jnp.maximum, lses)
            ws = [jnp.exp2(x - top) for x in lses]
            total = functools.reduce(jnp.add, ws)
            acc = jnp.zeros((TQ, HD), F32)
            for z in range(NZ):
                acc = acc + ws[z] * o_ref[p * NZ + z, 0:TQ, hs].astype(F32)
            attn_ref[p * TQ : (p + 1) * TQ, hs] = (acc / total).astype(BF)
    attn = attn_ref[...]
    copies = []
    for b in range(8):
        part = jnp.dot(attn, w_ref[:, b * W : (b + 1) * W], preferred_element_type=F32).astype(BF)
        out_ref[0, b] = part[0:TQ]
        out_ref[1, b] = part[TQ : 2 * TQ]
        copy = pltpu.make_async_copy(out_ref.at[:, b], out_hbm.at[:, b], sems.at[b])
        copy.start()
        copies.append(copy)
    for copy in copies:
        copy.wait()


def finish_kernel(ids, scal, part_ref, hid_ref, gate_ref, side_ref, bias_ref, lat_ref, guided_ref, next_ref):
    mine = ids[0]
    mine_f = mine.astype(F32)
    outs = []
    other_gate = (
        side_ref[TQ : TQ + 1, :].astype(F32) + side_ref[TQ + 1 : TQ + 2, :].astype(F32)
    ) + side_ref[TQ + 2 : TQ + 3, :].astype(F32)
    for g in range(2):
        acc = part_ref[g * 8].astype(F32)
        for b in range(1, 8):
            acc = acc + part_ref[g * 8 + b].astype(F32)
        own = mine == g
        hidden = jnp.where(own, hid_ref[mine].astype(F32), side_ref[0:TQ, :].astype(F32))
        gate = jnp.where(own, gate_ref[pl.ds(mine, 1), :], other_gate)
        outs.append((hidden + gate * (acc + bias_ref[...])).astype(BF).astype(F32))
    cond, uncond = outs
    guided = uncond + scal[0] * (cond - uncond)
    guided_ref[0] = guided.astype(BF)
    next_ref[0] = (lat_ref[0].astype(F32) + scal[1] * guided).astype(BF)


SMEM = functools.partial(pl.BlockSpec, memory_space=pltpu.SMEM)
VMEM = functools.partial(pl.BlockSpec, memory_space=pltpu.VMEM)
HBM = functools.partial(pl.BlockSpec, memory_space=pltpu.HBM)


def call(kernel, outs, ins, out_specs, name, scratch=(), limit=VMEM_LIMIT, cost=None):
    return pl.pallas_call(
        kernel,
        out_shape=outs,
        in_specs=ins,
        out_specs=out_specs,
        scratch_shapes=list(scratch),
        compiler_params=pltpu.CompilerParams(vmem_limit_bytes=limit),
        cost_estimate=cost,
        name=name,
    )


def shards(
    img_hidden,
    img_query,
    img_key,
    img_value,
    txt_key,
    txt_value,
    query_gain,
    key_gain,
    gate,
    proj_weight,
    proj_bias,
    guidance,
    text_len,
    step_index,
    latent,
):
    guide = lax.axis_index("g")
    xh = lax.axis_index("xh")
    z1 = lax.axis_index("z1")
    z0 = lax.axis_index("z0")
    seq = (xh * NZ + z1) * NZ + z0
    rows, cols = rope_tables()
    kv_shape = jax.ShapeDtypeStruct((2, TK, W), BF)
    keep, send, q, side = call(
        prepare_kernel,
        (kv_shape, kv_shape, jax.ShapeDtypeStruct((NS, TQ, W), BF), jax.ShapeDtypeStruct((TQ + 8, W), BF)),
        [SMEM()] * 3 + [HBM()] * 11,
        (VMEM(),) * 4,
        "prepare",
        [
            pltpu.VMEM((2, TQ, W), BF),
            pltpu.VMEM((2, TQ, W), BF),
            pltpu.VMEM((2, TQ, W), BF),
            pltpu.VMEM((2, TT, W), BF),
            pltpu.VMEM((2, TT, W), BF),
            pltpu.VMEM((TQ, W), BF),
            pltpu.VMEM((2, W), F32),
            pltpu.VMEM((1, HD), F32),
            pltpu.VMEM((2, HD), F32),
            pltpu.VMEM((2, 1, HD), F32),
            pltpu.VMEM((2, TQ, HD), F32),
            pltpu.SemaphoreType.DMA((11,)),
        ],
        63 * 1024 * 1024,
    )(
        seq[None],
        xh[None],
        guide[None],
        img_key[0],
        img_query[0],
        img_value[0],
        txt_key[0],
        txt_value[0],
        img_hidden[0],
        gate[0],
        query_gain[None],
        key_gain,
        jnp.asarray(rows),
        jnp.asarray(cols),
    )
    q = lax.all_to_all(q, ("xh", "z0"), 0, 0, tiled=True)
    swap = [(0, 1), (1, 0)]
    got = lax.ppermute(send, "xh", swap)
    kv = call(
        join_kernel,
        jax.ShapeDtypeStruct((2, 2, TK, W), BF),
        [VMEM()] * 2,
        VMEM(),
        "join",
        cost=pl.CostEstimate(flops=10**11, bytes_accessed=10**6, transcendentals=0),
    )(keep, got)
    kv = lax.all_gather(kv, "z1", axis=0)

    out = call(
        attend_kernel,
        jax.ShapeDtypeStruct((NS, TQ + STAT, W), BF),
        [SMEM()] * 3 + [VMEM()] * 2,
        VMEM(),
        "attend",
    )(xh[None], z0[None], text_len, q, kv)
    out, side = lax.optimization_barrier((out, side))
    side = lax.ppermute(side, "g", swap)
    out = lax.all_to_all(out, ("xh", "z0"), 0, 0, tiled=True)
    out, side = lax.optimization_barrier((out, side))
    part = call(
        project_kernel,
        jax.ShapeDtypeStruct((2, 8, TQ, W), BF),
        [SMEM()] + [VMEM()] * 2,
        HBM(),
        "project",
        [pltpu.VMEM((2 * TQ, W), BF), pltpu.VMEM((2, 8, TQ, W), BF), pltpu.SemaphoreType.DMA((8,))],
    )((z0 & 1)[None], out, proj_weight)
    part = lax.all_to_all(part.reshape(16, TQ, W), ("g", "y", "c"), 0, 0, tiled=True)
    index = step_index[0]
    u_now = 1.0 - index.astype(F32) / STEPS
    u_next = 1.0 - (index + 1).astype(F32) / STEPS
    step = 3.0 * u_next / (1.0 + 2.0 * u_next) - 3.0 * u_now / (1.0 + 2.0 * u_now)
    shape = jax.ShapeDtypeStruct((1, TQ, W), BF)
    return call(finish_kernel, (shape, shape), [SMEM()] * 2 + [VMEM()] * 6, (VMEM(),) * 2, "finish")(
        guide[None],
        jnp.stack([guidance[guide], step]),
        part,
        img_hidden[0],
        gate[0],
        side,
        proj_bias[None],
        latent,
    )


def solution(mesh):
    fine = Mesh(mesh.devices.reshape(2, 2, NZ, NZ, 4, 2), ("g", "xh", "z1", "z0", "y", "c"))
    seq = ("xh", "z1", "z0")
    blk = ("y", "c")
    act = P("g", None, seq, blk)
    return jax.shard_map(
        shards,
        mesh=fine,
        in_specs=(
            act,
            act,
            act,
            act,
            act,
            act,
            P(),
            P(),
            P("g", None, blk),
            P(blk, None),
            P(blk),
            P(),
            P(),
            P(),
            P("g", seq, blk),
        ),
        out_specs=(P("g", seq, blk), P("g", seq, blk)),
        check_vma=False,
    )
```

```python
import functools

import jax
import jax.numpy as jnp
import numpy as np
from jax import lax
from jax.experimental import pallas as pl
from jax.experimental.pallas import tpu as pltpu
from jax.sharding import Mesh, PartitionSpec as P

HD = 128
GRID = 64
STEPS = 8
HPD = 3
W = HPD * HD
TQ = 64
TT = 16
TK = TQ + TT
NZ = 4
NS = 8
STAT = 8
BF = jnp.bfloat16
F32 = jnp.float32
VMEM_LIMIT = 48 * 1024 * 1024


def rope_tables():
    first = HD // 8
    second = (HD - first) // 2
    freqs = 10000.0 ** (-np.arange(0, second, 2).astype(np.float64) / second)
    n = freqs.shape[0]
    lane = np.arange(HD)
    pair = lane // 2
    sign = np.where(lane % 2 == 0, -1.0, 1.0)
    row_f = np.where((pair >= first // 2) & (pair < first // 2 + n), freqs[np.clip(pair - first // 2, 0, n - 1)], 0.0)
    col_f = np.where(pair >= first // 2 + n, freqs[np.clip(pair - first // 2 - n, 0, n - 1)], 0.0)
    rows = np.arange(32)[:, None] * row_f[None]
    cols = np.arange(GRID)[:, None] * col_f[None]
    return (
        np.stack([np.cos(rows), np.sin(rows) * sign]).astype(np.float32),
        np.stack([np.cos(cols), np.sin(cols) * sign]).astype(np.float32),
    )


def split3(x):
    hi = x.astype(BF)
    rest = x - hi.astype(F32)
    mid = rest.astype(BF)
    lo = (rest - mid.astype(F32)).astype(BF)
    return hi, mid, lo


def rope_of(row_ref, col_ref):
    in_row = lax.broadcasted_iota(jnp.int32, (TQ, HD), 1) < 72
    return jnp.where(in_row, row_ref[0], col_ref[0]), jnp.where(in_row, row_ref[1], col_ref[1])


def normed(x, gain):
    x = x.astype(F32)
    return x * lax.rsqrt(jnp.mean(x * x, -1, keepdims=True) + 1e-06) * gain


def rotated(x, table):
    even = lax.broadcasted_iota(jnp.int32, (TQ, HD), 1) % 2 == 0
    swapped = jnp.where(even, pltpu.roll(x, HD - 1, 1), pltpu.roll(x, 1, 1))
    return x * table[0] + swapped * table[1]


def start_all(pairs, sems):
    copies = [pltpu.make_async_copy(src, dst, sems.at[i]) for i, (src, dst) in enumerate(pairs)]
    for copy in copies:
        copy.start()
    return copies


def prepare_kernel(
    seq_id, xh_id, guide_id, k_hbm, q_hbm, v_hbm, tk_hbm, tv_hbm, hid_hbm, gate_hbm, qg_hbm, kg_hbm, row_hbm, col_hbm,
    keep_out, send_out, q_out, side_out,
    k_ref, q_ref, v_ref, tk_ref, tv_ref, hid_ref, gate_ref, qg_ref, kg_ref, row_ref, col_ref, sems,
):
    other = 1 - guide_id[0]
    rows = row_hbm.at[:, pl.ds(seq_id[0], 1)]
    copies = start_all(
        (
            (rows, row_ref), (col_hbm, col_ref), (qg_hbm, qg_ref), (q_hbm, q_ref), (kg_hbm, kg_ref), (tk_hbm, tk_ref), (k_hbm, k_ref),
            (v_hbm, v_ref), (tv_hbm, tv_ref), (hid_hbm.at[other], hid_ref), (gate_hbm, gate_ref),
        ),
        sems,
    )
    for copy in copies[:4]:
        copy.wait()
    table = rope_of(row_ref, col_ref)
    for p in range(2):
        for h in range(HPD):
            hs = slice(h * HD, (h + 1) * HD)
            q = rotated(normed(q_ref[p, :, hs], qg_ref[...]), table).astype(BF)
            for z in range(NZ):
                q_out[p * NZ + z, :, hs] = q
    for copy in copies[4:7]:
        copy.wait()
    own = xh_id[0]
    for out, p in ((keep_out.at[0], own), (send_out, 1 - own)):
        for h in range(HPD):
            hs = slice(h * HD, (h + 1) * HD)
            out[0, 0:TT, hs] = normed(tk_ref[p, :, hs], kg_ref[1:2]).astype(BF)
            out[0, TT:TK, hs] = rotated(normed(k_ref[p, :, hs], kg_ref[0:1]), table).astype(BF)
    for copy in copies[7:]:
        copy.wait()
    for out, p in ((keep_out.at[0], own), (send_out, 1 - own)):
        out[1, 0:TT, :] = tv_ref[p]
        out[1, TT:TK, :] = v_ref[p]
    side_out[0:TQ, :] = hid_ref[...]
    hi, mid, lo = split3(gate_ref[pl.ds(other, 1), :])
    rows = lax.broadcasted_iota(jnp.int32, (8, W), 0)
    packed = jnp.where(rows == 0, hi.astype(F32), jnp.where(rows == 1, mid.astype(F32), lo.astype(F32)))
    side_out[TQ : TQ + 8, :] = packed.astype(BF)


def join_kernel(kv_hbm, got_hbm, out_hbm, sem):
    del kv_hbm
    copy = pltpu.make_async_copy(got_hbm, out_hbm.at[1], sem)
    copy.start()
    copy.wait()


def attend_kernel(xh_id, z0_id, len_ref, q_ref, kv_ref, out_ref):
    scale = HD ** (-0.5) * 1.4426950408889634
    own = xh_id[0]
    at = lax.broadcasted_iota(jnp.int32, (1, NS * TK), 1)
    block = jnp.zeros_like(at)
    for i in range(1, NS):
        block = block + (at >= i * TK).astype(jnp.int32)
    within = at - block * TK
    from_own = (block & 1) == 0
    seq = (jnp.where(from_own, own, 1 - own) * NZ + (block >> 1)) * NZ + z0_id[0]
    dead = (within < TT) & (seq * TT + within >= len_ref[own])
    bias = jnp.where(dead, -1e30, 0.0)
    lane = lax.broadcasted_iota(jnp.int32, (NS * TQ, HD), 1)
    stats = jnp.zeros((NS * TQ, HD), F32)
    for h in range(HPD):
        hs = slice(h * HD, (h + 1) * HD)
        q = q_ref[:, :, hs].reshape(NS * TQ, HD)
        k = kv_ref[:, :, 0, :, hs].reshape(NS * TK, HD)
        v = kv_ref[:, :, 1, :, hs].reshape(NS * TK, HD)
        s = lax.dot_general(q, k, (((1,), (1,)), ((), ())), preferred_element_type=F32)
        s = s * scale + bias
        top = jnp.max(s, -1, keepdims=True)
        e = jnp.exp2(s - top)
        total = jnp.sum(e, -1, keepdims=True)
        o = jnp.dot(e.astype(BF), v, preferred_element_type=F32) / total
        out_ref[:, 0:TQ, hs] = o.astype(BF).reshape(NS, TQ, HD)
        lse = top + jnp.log2(total)
        hi = lse.astype(BF).astype(F32)
        stats = jnp.where(lane == h, hi, jnp.where(lane == HPD + h, lse - hi, stats))
    rows = jnp.transpose(stats)[0:STAT, :].astype(BF)
    for d in range(NS):
        a = (d // 2) * HD
        out_ref[d, TQ : TQ + STAT, 0:HD] = rows[:, a : a + HD]
        out_ref[d, TQ : TQ + STAT, HD:W] = jnp.zeros((STAT, W - HD), BF)


def project_kernel(ids, o_ref, w_ref, out_hbm, attn_ref, out_ref, sems):
    odd = ids[0]
    stats = o_ref[:, TQ : TQ + STAT, 0:HD].astype(F32).reshape(NS * STAT, HD)
    cols = jnp.transpose(jnp.concatenate([stats, stats], 0))
    cols = jnp.where(odd == 0, cols[0:TQ], cols[TQ : 2 * TQ])
    for p in range(2):
        for h in range(HPD):
            hs = slice(h * HD, (h + 1) * HD)
            lses = []
            for z in range(NZ):
                at = (p * NZ + z) * STAT + h
                lses.append(cols[:, at : at + 1] + cols[:, at + HPD : at + HPD + 1])
            top = functools.reduce(jnp.maximum, lses)
            ws = [jnp.exp2(x - top) for x in lses]
            total = functools.reduce(jnp.add, ws)
            acc = jnp.zeros((TQ, HD), F32)
            for z in range(NZ):
                acc = acc + ws[z] * o_ref[p * NZ + z, 0:TQ, hs].astype(F32)
            attn_ref[p * TQ : (p + 1) * TQ, hs] = (acc / total).astype(BF)
    attn = attn_ref[...]
    copies = []
    for b in range(8):
        part = jnp.dot(attn, w_ref[:, b * W : (b + 1) * W], preferred_element_type=F32).astype(BF)
        out_ref[0, b] = part[0:TQ]
        out_ref[1, b] = part[TQ : 2 * TQ]
        copy = pltpu.make_async_copy(out_ref.at[:, b], out_hbm.at[:, b], sems.at[b])
        copy.start()
        copies.append(copy)
    for copy in copies:
        copy.wait()


def finish_kernel(ids, scal, part_ref, hid_ref, gate_ref, side_ref, bias_ref, lat_ref, guided_ref, next_ref):
    mine = ids[0]
    mine_f = mine.astype(F32)
    outs = []
    other_gate = (
        side_ref[TQ : TQ + 1, :].astype(F32) + side_ref[TQ + 1 : TQ + 2, :].astype(F32)
    ) + side_ref[TQ + 2 : TQ + 3, :].astype(F32)
    for g in range(2):
        acc = part_ref[g * 8].astype(F32)
        for b in range(1, 8):
            acc = acc + part_ref[g * 8 + b].astype(F32)
        own = mine == g
        hidden = jnp.where(own, hid_ref[mine].astype(F32), side_ref[0:TQ, :].astype(F32))
        gate = jnp.where(own, gate_ref[pl.ds(mine, 1), :], other_gate)
        outs.append((hidden + gate * (acc + bias_ref[...])).astype(BF).astype(F32))
    cond, uncond = outs
    guided = uncond + scal[0] * (cond - uncond)
    guided_ref[0] = guided.astype(BF)
    next_ref[0] = (lat_ref[0].astype(F32) + scal[1] * guided).astype(BF)


SMEM = functools.partial(pl.BlockSpec, memory_space=pltpu.SMEM)
VMEM = functools.partial(pl.BlockSpec, memory_space=pltpu.VMEM)
HBM = functools.partial(pl.BlockSpec, memory_space=pltpu.HBM)


def call(kernel, outs, ins, out_specs, name, scratch=(), limit=VMEM_LIMIT, cost=None, aliases={}):
    return pl.pallas_call(
        kernel,
        out_shape=outs,
        in_specs=ins,
        out_specs=out_specs,
        scratch_shapes=list(scratch),
        compiler_params=pltpu.CompilerParams(vmem_limit_bytes=limit),
        cost_estimate=cost,
        input_output_aliases=aliases,
        name=name,
    )


def shards(
    img_hidden,
    img_query,
    img_key,
    img_value,
    txt_key,
    txt_value,
    query_gain,
    key_gain,
    gate,
    proj_weight,
    proj_bias,
    guidance,
    text_len,
    step_index,
    latent,
):
    guide = lax.axis_index("g")
    xh = lax.axis_index("xh")
    z1 = lax.axis_index("z1")
    z0 = lax.axis_index("z0")
    seq = (xh * NZ + z1) * NZ + z0
    rows, cols = rope_tables()
    keep, send, q, side = call(
        prepare_kernel,
        (
            jax.ShapeDtypeStruct((2, 2, TK, W), BF),
            jax.ShapeDtypeStruct((2, TK, W), BF),
            jax.ShapeDtypeStruct((NS, TQ, W), BF),
            jax.ShapeDtypeStruct((TQ + 8, W), BF),
        ),
        [SMEM()] * 3 + [HBM()] * 11,
        (VMEM(),) * 4,
        "prepare",
        [
            pltpu.VMEM((2, TQ, W), BF),
            pltpu.VMEM((2, TQ, W), BF),
            pltpu.VMEM((2, TQ, W), BF),
            pltpu.VMEM((2, TT, W), BF),
            pltpu.VMEM((2, TT, W), BF),
            pltpu.VMEM((TQ, W), BF),
            pltpu.VMEM((2, W), F32),
            pltpu.VMEM((1, HD), F32),
            pltpu.VMEM((2, HD), F32),
            pltpu.VMEM((2, 1, HD), F32),
            pltpu.VMEM((2, TQ, HD), F32),
            pltpu.SemaphoreType.DMA((11,)),
        ],
        63 * 1024 * 1024,
    )(
        seq[None],
        xh[None],
        guide[None],
        img_key[0],
        img_query[0],
        img_value[0],
        txt_key[0],
        txt_value[0],
        img_hidden[0],
        gate[0],
        query_gain[None],
        key_gain,
        jnp.asarray(rows),
        jnp.asarray(cols),
    )
    q = lax.all_to_all(q, ("xh", "z0"), 0, 0, tiled=True)
    swap = [(0, 1), (1, 0)]
    got = lax.ppermute(send, "xh", swap)
    kv = call(
        join_kernel,
        pltpu.HBM((2, 2, TK, W), BF),
        [HBM()] * 2,
        HBM(),
        "join",
        [pltpu.SemaphoreType.DMA],
        cost=pl.CostEstimate(flops=10**11, bytes_accessed=10**6, transcendentals=0),
        aliases={0: 0},
    )(keep, got)
    kv = lax.all_gather(kv, "z1", axis=0)

    out = call(
        attend_kernel,
        pltpu.HBM((NS, TQ + STAT, W), BF),
        [SMEM()] * 3 + [VMEM()] * 2,
        VMEM(),
        "attend",
    )(xh[None], z0[None], text_len, q, kv)
    out, side = lax.optimization_barrier((out, side))
    side = lax.ppermute(side, "g", swap)
    out = lax.all_to_all(out, ("xh", "z0"), 0, 0, tiled=True)
    out, side = lax.optimization_barrier((out, side))
    part = call(
        project_kernel,
        jax.ShapeDtypeStruct((2, 8, TQ, W), BF),
        [SMEM()] + [VMEM()] * 2,
        HBM(),
        "project",
        [pltpu.VMEM((2 * TQ, W), BF), pltpu.VMEM((2, 8, TQ, W), BF), pltpu.SemaphoreType.DMA((8,))],
    )((z0 & 1)[None], out, proj_weight)
    part = lax.all_to_all(part.reshape(16, TQ, W), ("g", "y", "c"), 0, 0, tiled=True)
    index = step_index[0]
    u_now = 1.0 - index.astype(F32) / STEPS
    u_next = 1.0 - (index + 1).astype(F32) / STEPS
    step = 3.0 * u_next / (1.0 + 2.0 * u_next) - 3.0 * u_now / (1.0 + 2.0 * u_now)
    shape = jax.ShapeDtypeStruct((1, TQ, W), BF)
    return call(finish_kernel, (shape, shape), [SMEM()] * 2 + [VMEM()] * 6, (VMEM(),) * 2, "finish")(
        guide[None],
        jnp.stack([guidance[guide], step]),
        part,
        img_hidden[0],
        gate[0],
        side,
        proj_bias[None],
        latent,
    )


def solution(mesh):
    fine = Mesh(mesh.devices.reshape(2, 2, NZ, NZ, 4, 2), ("g", "xh", "z1", "z0", "y", "c"))
    seq = ("xh", "z1", "z0")
    blk = ("y", "c")
    act = P("g", None, seq, blk)
    return jax.shard_map(
        shards,
        mesh=fine,
        in_specs=(
            act,
            act,
            act,
            act,
            act,
            act,
            P(),
            P(),
            P("g", None, blk),
            P(blk, None),
            P(blk),
            P(),
            P(),
            P(),
            P("g", seq, blk),
        ),
        out_specs=(P("g", seq, blk), P("g", seq, blk)),
        check_vma=False,
    )
```

```python
import functools

import jax
import jax.numpy as jnp
import numpy as np
from jax import lax
from jax.experimental import pallas as pl
from jax.experimental.pallas import tpu as pltpu
from jax.sharding import Mesh, PartitionSpec as P

HD = 128
GRID = 64
STEPS = 8
HPD = 3
W = HPD * HD
TQ = 64
TT = 16
TK = TQ + TT
NK = 8
NQ = 2
NS = 2 * NQ
NB = 2 * NK
STAT = 8
VR = 2 * TT + TQ
BF = jnp.bfloat16
F32 = jnp.float32
VMEM_LIMIT = 48 * 1024 * 1024


def rope_tables():
    first = HD // 8
    second = (HD - first) // 2
    freqs = 10000.0 ** (-np.arange(0, second, 2).astype(np.float64) / second)
    n = freqs.shape[0]
    lane = np.arange(HD)
    pair = lane // 2
    sign = np.where(lane % 2 == 0, -1.0, 1.0)
    row_f = np.where((pair >= first // 2) & (pair < first // 2 + n), freqs[np.clip(pair - first // 2, 0, n - 1)], 0.0)
    col_f = np.where(pair >= first // 2 + n, freqs[np.clip(pair - first // 2 - n, 0, n - 1)], 0.0)
    rows = np.arange(32)[:, None] * row_f[None]
    cols = np.arange(GRID)[:, None] * col_f[None]
    return (
        np.stack([np.cos(rows), np.sin(rows) * sign]).astype(np.float32),
        np.stack([np.cos(cols), np.sin(cols) * sign]).astype(np.float32),
    )


def split3(x):
    hi = x.astype(BF)
    rest = x - hi.astype(F32)
    mid = rest.astype(BF)
    lo = (rest - mid.astype(F32)).astype(BF)
    return hi, mid, lo


def rope_of(row_ref, col_ref):
    in_row = lax.broadcasted_iota(jnp.int32, (TQ, HD), 1) < 72
    return jnp.where(in_row, row_ref[0], col_ref[0]), jnp.where(in_row, row_ref[1], col_ref[1])


def normed(x, gain):
    x = x.astype(F32)
    return x * lax.rsqrt(jnp.mean(x * x, -1, keepdims=True) + 1e-06) * gain


def rotated(x, table):
    even = lax.broadcasted_iota(jnp.int32, (TQ, HD), 1) % 2 == 0
    swapped = jnp.where(even, pltpu.roll(x, HD - 1, 1), pltpu.roll(x, 1, 1))
    return x * table[0] + swapped * table[1]


def start_all(pairs, sems):
    copies = [pltpu.make_async_copy(src, dst, sems.at[i]) for i, (src, dst) in enumerate(pairs)]
    for copy in copies:
        copy.start()
    return copies


def prepare_kernel(
    seq_id, xh_id, guide_id, k_hbm, q_hbm, v_hbm, tk_hbm, tv_hbm, hid_hbm, gate_hbm, qg_hbm, kg_hbm, row_hbm, col_hbm,
    keep_v, keep_k, send_out, q_out, side_out,
    k_ref, q_ref, v_ref, tk_ref, tv_ref, hid_ref, gate_ref, qg_ref, kg_ref, row_ref, col_ref, sems,
):
    other = 1 - guide_id[0]
    rows = row_hbm.at[:, pl.ds(seq_id[0], 1)]
    copies = start_all(
        (
            (rows, row_ref), (col_hbm, col_ref), (qg_hbm, qg_ref), (q_hbm, q_ref), (kg_hbm, kg_ref), (tk_hbm, tk_ref), (k_hbm, k_ref),
            (v_hbm, v_ref), (tv_hbm, tv_ref), (hid_hbm.at[other], hid_ref), (gate_hbm, gate_ref),
        ),
        sems,
    )
    for copy in copies[:4]:
        copy.wait()
    table = rope_of(row_ref, col_ref)
    for p in range(2):
        for h in range(HPD):
            hs = slice(h * HD, (h + 1) * HD)
            q = rotated(normed(q_ref[p, :, hs], qg_ref[...]), table).astype(BF)
            for z in range(NQ):
                q_out[p * NQ + z, :, hs] = q
    for copy in copies[4:7]:
        copy.wait()
    own = xh_id[0]
    vals = ((keep_v.at[0], own), (send_out.at[0:VR], 1 - own))
    imgs = ((keep_k.at[0], own), (send_out.at[VR:], 1 - own))
    for h in range(HPD):
        hs = slice(h * HD, (h + 1) * HD)
        for out, p in vals:
            out[0:TT, hs] = normed(tk_ref[p, :, hs], kg_ref[1:2]).astype(BF)
        for out, p in imgs:
            out[:, hs] = rotated(normed(k_ref[p, :, hs], kg_ref[0:1]), table).astype(BF)
    for copy in copies[7:]:
        copy.wait()
    for out, p in vals:
        out[TT : 2 * TT, :] = tv_ref[p]
        out[2 * TT :, :] = v_ref[p]
    side_out[0:TQ, :] = hid_ref[...]
    hi, mid, lo = split3(gate_ref[pl.ds(other, 1), :])
    rows = lax.broadcasted_iota(jnp.int32, (8, W), 0)
    packed = jnp.where(rows == 0, hi.astype(F32), jnp.where(rows == 1, mid.astype(F32), lo.astype(F32)))
    side_out[TQ : TQ + 8, :] = packed.astype(BF)


def join_kernel(v_in, k_in, got_hbm, v_out, k_out, sems):
    del v_in, k_in
    for copy in start_all(((got_hbm.at[0:VR], v_out.at[1]), (got_hbm.at[VR:], k_out.at[1])), sems):
        copy.wait()


def attend_kernel(xh_id, z0_id, len_ref, q_ref, v_ref, k_ref, out_ref):
    scale = HD ** (-0.5) * 1.4426950408889634
    own = xh_id[0]
    at = lax.broadcasted_iota(jnp.int32, (1, NB * TT), 1)
    block = at >> 4
    seq = (jnp.where((block & 1) == 0, own, 1 - own) * NK + (block >> 1)) * NQ + z0_id[0]
    bias = jnp.where(seq * TT + (at & 15) >= len_ref[own], -1e30, 0.0)
    lane = lax.broadcasted_iota(jnp.int32, (NS * TQ, HD), 1)
    stats = jnp.zeros((NS * TQ, HD), F32)
    for h in range(HPD):
        hs = slice(h * HD, (h + 1) * HD)
        q = q_ref[:, :, hs].reshape(NS * TQ, HD)
        kt = v_ref[:, 0:TT, hs].reshape(NB * TT, HD)
        vt = v_ref[:, TT : 2 * TT, hs].reshape(NB * TT, HD)
        ki = k_ref[:, :, hs].reshape(NB * TQ, HD)
        vi = v_ref[:, 2 * TT :, hs].reshape(NB * TQ, HD)
        dims = (((1,), (1,)), ((), ()))
        st = lax.dot_general(q, kt, dims, preferred_element_type=F32) * scale + bias
        si = lax.dot_general(q, ki, dims, preferred_element_type=F32) * scale
        top = jnp.maximum(jnp.max(st, -1, keepdims=True), jnp.max(si, -1, keepdims=True))
        et = jnp.exp2(st - top)
        ei = jnp.exp2(si - top)
        total = jnp.sum(et, -1, keepdims=True) + jnp.sum(ei, -1, keepdims=True)
        o = jnp.dot(ei.astype(BF), vi, preferred_element_type=F32)
        o = (o + jnp.dot(et.astype(BF), vt, preferred_element_type=F32)) / total
        out_ref[:, 0:TQ, hs] = o.astype(BF).reshape(NS, TQ, HD)
        lse = top + jnp.log2(total)
        hi = lse.astype(BF).astype(F32)
        stats = jnp.where(lane == h, hi, jnp.where(lane == HPD + h, lse - hi, stats))
    rows = jnp.transpose(stats)[0:STAT, :].astype(BF)
    for d in range(NS):
        a = (d // 2) * HD
        out_ref[d, TQ : TQ + STAT, 0:HD] = rows[:, a : a + HD]
        out_ref[d, TQ : TQ + STAT, HD:W] = jnp.zeros((STAT, W - HD), BF)


def project_kernel(ids, o_ref, w_ref, out_hbm, attn_ref, out_ref, sems):
    odd = ids[0]
    stats = o_ref[:, TQ : TQ + STAT, 0:HD].astype(F32).reshape(NS * STAT, HD)
    cols = jnp.transpose(jnp.concatenate([stats] * (HD // (NS * STAT)), 0))
    cols = jnp.where(odd == 0, cols[0:TQ], cols[TQ : 2 * TQ])
    for p in range(2):
        for h in range(HPD):
            hs = slice(h * HD, (h + 1) * HD)
            lses = []
            for z in range(NQ):
                at = (p * NQ + z) * STAT + h
                lses.append(cols[:, at : at + 1] + cols[:, at + HPD : at + HPD + 1])
            top = functools.reduce(jnp.maximum, lses)
            ws = [jnp.exp2(x - top) for x in lses]
            total = functools.reduce(jnp.add, ws)
            acc = jnp.zeros((TQ, HD), F32)
            for z in range(NQ):
                acc = acc + ws[z] * o_ref[p * NQ + z, 0:TQ, hs].astype(F32)
            attn_ref[p * TQ : (p + 1) * TQ, hs] = (acc / total).astype(BF)
    attn = attn_ref[...]
    copies = []
    for b in range(8):
        part = jnp.dot(attn, w_ref[:, b * W : (b + 1) * W], preferred_element_type=F32).astype(BF)
        out_ref[0, b] = part[0:TQ]
        out_ref[1, b] = part[TQ : 2 * TQ]
        copy = pltpu.make_async_copy(out_ref.at[:, b], out_hbm.at[:, b], sems.at[b])
        copy.start()
        copies.append(copy)
    for copy in copies:
        copy.wait()


def finish_kernel(ids, scal, part_ref, hid_ref, gate_ref, side_ref, bias_ref, lat_ref, guided_ref, next_ref):
    mine = ids[0]
    mine_f = mine.astype(F32)
    outs = []
    other_gate = (
        side_ref[TQ : TQ + 1, :].astype(F32) + side_ref[TQ + 1 : TQ + 2, :].astype(F32)
    ) + side_ref[TQ + 2 : TQ + 3, :].astype(F32)
    for g in range(2):
        acc = part_ref[g * 8].astype(F32)
        for b in range(1, 8):
            acc = acc + part_ref[g * 8 + b].astype(F32)
        own = mine == g
        hidden = jnp.where(own, hid_ref[mine].astype(F32), side_ref[0:TQ, :].astype(F32))
        gate = jnp.where(own, gate_ref[pl.ds(mine, 1), :], other_gate)
        outs.append((hidden + gate * (acc + bias_ref[...])).astype(BF).astype(F32))
    cond, uncond = outs
    guided = uncond + scal[0] * (cond - uncond)
    guided_ref[0] = guided.astype(BF)
    next_ref[0] = (lat_ref[0].astype(F32) + scal[1] * guided).astype(BF)


SMEM = functools.partial(pl.BlockSpec, memory_space=pltpu.SMEM)
VMEM = functools.partial(pl.BlockSpec, memory_space=pltpu.VMEM)
HBM = functools.partial(pl.BlockSpec, memory_space=pltpu.HBM)


def call(kernel, outs, ins, out_specs, name, scratch=(), limit=VMEM_LIMIT, cost=None, aliases={}):
    return pl.pallas_call(
        kernel,
        out_shape=outs,
        in_specs=ins,
        out_specs=out_specs,
        scratch_shapes=list(scratch),
        compiler_params=pltpu.CompilerParams(vmem_limit_bytes=limit),
        cost_estimate=cost,
        input_output_aliases=aliases,
        name=name,
    )


def shards(
    img_hidden,
    img_query,
    img_key,
    img_value,
    txt_key,
    txt_value,
    query_gain,
    key_gain,
    gate,
    proj_weight,
    proj_bias,
    guidance,
    text_len,
    step_index,
    latent,
):
    guide = lax.axis_index("g")
    xh = lax.axis_index("xh")
    z1 = lax.axis_index("z1")
    z0 = lax.axis_index("z0")
    seq = (xh * NK + z1) * NQ + z0
    rows, cols = rope_tables()
    keep_v, keep_k, send, q, side = call(
        prepare_kernel,
        (
            jax.ShapeDtypeStruct((2, VR, W), BF),
            jax.ShapeDtypeStruct((2, TQ, W), BF),
            jax.ShapeDtypeStruct((VR + TQ, W), BF),
            jax.ShapeDtypeStruct((NS, TQ, W), BF),
            jax.ShapeDtypeStruct((TQ + 8, W), BF),
        ),
        [SMEM()] * 3 + [HBM()] * 11,
        (VMEM(),) * 5,
        "prepare",
        [
            pltpu.VMEM((2, TQ, W), BF),
            pltpu.VMEM((2, TQ, W), BF),
            pltpu.VMEM((2, TQ, W), BF),
            pltpu.VMEM((2, TT, W), BF),
            pltpu.VMEM((2, TT, W), BF),
            pltpu.VMEM((TQ, W), BF),
            pltpu.VMEM((2, W), F32),
            pltpu.VMEM((1, HD), F32),
            pltpu.VMEM((2, HD), F32),
            pltpu.VMEM((2, 1, HD), F32),
            pltpu.VMEM((2, TQ, HD), F32),
            pltpu.SemaphoreType.DMA((11,)),
        ],
        63 * 1024 * 1024,
    )(
        seq[None],
        xh[None],
        guide[None],
        img_key[0],
        img_query[0],
        img_value[0],
        txt_key[0],
        txt_value[0],
        img_hidden[0],
        gate[0],
        query_gain[None],
        key_gain,
        jnp.asarray(rows),
        jnp.asarray(cols),
    )
    q = lax.all_to_all(q, ("xh", "z0"), 0, 0, tiled=True)
    swap = [(0, 1), (1, 0)]
    got = lax.ppermute(send, "xh", swap)
    v, k = call(
        join_kernel,
        (pltpu.HBM((2, VR, W), BF), pltpu.HBM((2, TQ, W), BF)),
        [HBM()] * 3,
        (HBM(),) * 2,
        "join",
        [pltpu.SemaphoreType.DMA((2,))],
        cost=pl.CostEstimate(flops=10**11, bytes_accessed=10**6, transcendentals=0),
        aliases={0: 0, 1: 1},
    )(keep_v, keep_k, got)
    v = lax.all_gather(v, "z1", axis=0, tiled=True)
    k = lax.all_gather(k, "z1", axis=0, tiled=True)

    out = call(
        attend_kernel,
        pltpu.HBM((NS, TQ + STAT, W), BF),
        [SMEM()] * 3 + [VMEM()] * 3,
        VMEM(),
        "attend",
    )(xh[None], z0[None], text_len, q, v, k)
    out, side = lax.optimization_barrier((out, side))
    side = lax.ppermute(side, "g", swap)
    out = lax.all_to_all(out, ("xh", "z0"), 0, 0, tiled=True)
    out, side = lax.optimization_barrier((out, side))
    part = call(
        project_kernel,
        jax.ShapeDtypeStruct((2, 8, TQ, W), BF),
        [SMEM()] + [VMEM()] * 2,
        HBM(),
        "project",
        [pltpu.VMEM((2 * TQ, W), BF), pltpu.VMEM((2, 8, TQ, W), BF), pltpu.SemaphoreType.DMA((8,))],
    )((z0 & 1)[None], out, proj_weight)
    part = lax.all_to_all(part.reshape(16, TQ, W), ("g", "y", "c"), 0, 0, tiled=True)
    index = step_index[0]
    u_now = 1.0 - index.astype(F32) / STEPS
    u_next = 1.0 - (index + 1).astype(F32) / STEPS
    step = 3.0 * u_next / (1.0 + 2.0 * u_next) - 3.0 * u_now / (1.0 + 2.0 * u_now)
    shape = jax.ShapeDtypeStruct((1, TQ, W), BF)
    return call(finish_kernel, (shape, shape), [SMEM()] * 2 + [VMEM()] * 6, (VMEM(),) * 2, "finish")(
        guide[None],
        jnp.stack([guidance[guide], step]),
        part,
        img_hidden[0],
        gate[0],
        side,
        proj_bias[None],
        latent,
    )


def solution(mesh):
    fine = Mesh(mesh.devices.reshape(2, 2, NK, NQ, 4, 2), ("g", "xh", "z1", "z0", "y", "c"))
    seq = ("xh", "z1", "z0")
    blk = ("y", "c")
    act = P("g", None, seq, blk)
    return jax.shard_map(
        shards,
        mesh=fine,
        in_specs=(
            act,
            act,
            act,
            act,
            act,
            act,
            P(),
            P(),
            P("g", None, blk),
            P(blk, None),
            P(blk),
            P(),
            P(),
            P(),
            P("g", seq, blk),
        ),
        out_specs=(P("g", seq, blk), P("g", seq, blk)),
        check_vma=False,
    )
```

```python
import functools

import jax
import jax.numpy as jnp
import numpy as np
from jax import lax
from jax.experimental import pallas as pl
from jax.experimental.pallas import tpu as pltpu
from jax.sharding import Mesh, PartitionSpec as P

HD = 128
GRID = 64
STEPS = 8
HPD = 3
W = HPD * HD
TQ = 64
TT = 16
TK = TQ + TT
NZ = 4
NS = 8
STAT = 8
BF = jnp.bfloat16
F32 = jnp.float32
VMEM_LIMIT = 48 * 1024 * 1024


def rope_tables():
    first = HD // 8
    second = (HD - first) // 2
    freqs = 10000.0 ** (-np.arange(0, second, 2).astype(np.float64) / second)
    n = freqs.shape[0]
    lane = np.arange(HD)
    pair = lane // 2
    sign = np.where(lane % 2 == 0, -1.0, 1.0)
    row_f = np.where((pair >= first // 2) & (pair < first // 2 + n), freqs[np.clip(pair - first // 2, 0, n - 1)], 0.0)
    col_f = np.where(pair >= first // 2 + n, freqs[np.clip(pair - first // 2 - n, 0, n - 1)], 0.0)
    rows = np.arange(32)[:, None] * row_f[None]
    cols = np.arange(GRID)[:, None] * col_f[None]
    return (
        np.stack([np.cos(rows), np.sin(rows) * sign]).astype(np.float32),
        np.stack([np.cos(cols), np.sin(cols) * sign]).astype(np.float32),
    )


def split3(x):
    hi = x.astype(BF)
    rest = x - hi.astype(F32)
    mid = rest.astype(BF)
    lo = (rest - mid.astype(F32)).astype(BF)
    return hi, mid, lo


def rope_of(row_ref, col_ref):
    in_row = lax.broadcasted_iota(jnp.int32, (TQ, HD), 1) < 72
    return jnp.where(in_row, row_ref[0], col_ref[0]), jnp.where(in_row, row_ref[1], col_ref[1])


def normed(x, gain):
    x = x.astype(F32)
    return x * lax.rsqrt(jnp.mean(x * x, -1, keepdims=True) + 1e-06) * gain


def rotated(x, table):
    even = lax.broadcasted_iota(jnp.int32, (TQ, HD), 1) % 2 == 0
    swapped = jnp.where(even, pltpu.roll(x, HD - 1, 1), pltpu.roll(x, 1, 1))
    return x * table[0] + swapped * table[1]


def start_all(pairs, sems):
    copies = [pltpu.make_async_copy(src, dst, sems.at[i]) for i, (src, dst) in enumerate(pairs)]
    for copy in copies:
        copy.start()
    return copies


def prepare_kernel(
    seq_id, xh_id, guide_id, k_hbm, q_hbm, v_hbm, tk_hbm, tv_hbm, hid_hbm, gate_hbm, qg_hbm, kg_hbm, row_hbm, col_hbm,
    keep_out, send_out, q_out, side_out,
    k_ref, q_ref, v_ref, tk_ref, tv_ref, hid_ref, gate_ref, qg_ref, kg_ref, row_ref, col_ref, sems,
):
    other = 1 - guide_id[0]
    rows = row_hbm.at[:, pl.ds(seq_id[0], 1)]
    copies = start_all(
        (
            (rows, row_ref), (col_hbm, col_ref), (qg_hbm, qg_ref), (q_hbm, q_ref), (kg_hbm, kg_ref), (tk_hbm, tk_ref), (k_hbm, k_ref),
            (v_hbm, v_ref), (tv_hbm, tv_ref), (hid_hbm.at[other], hid_ref), (gate_hbm, gate_ref),
        ),
        sems,
    )
    for copy in copies[:4]:
        copy.wait()
    table = rope_of(row_ref, col_ref)
    for p in range(2):
        for h in range(HPD):
            hs = slice(h * HD, (h + 1) * HD)
            q = rotated(normed(q_ref[p, :, hs], qg_ref[...]), table).astype(BF)
            for z in range(NZ):
                q_out[p * NZ + z, :, hs] = q
    for copy in copies[4:7]:
        copy.wait()
    own = xh_id[0]
    for out, p in ((keep_out.at[0], own), (send_out, 1 - own)):
        for h in range(HPD):
            hs = slice(h * HD, (h + 1) * HD)
            out[0, 0:TT, hs] = normed(tk_ref[p, :, hs], kg_ref[1:2]).astype(BF)
            out[0, TT:TK, hs] = rotated(normed(k_ref[p, :, hs], kg_ref[0:1]), table).astype(BF)
    for copy in copies[7:]:
        copy.wait()
    for out, p in ((keep_out.at[0], own), (send_out, 1 - own)):
        out[1, 0:TT, :] = tv_ref[p]
        out[1, TT:TK, :] = v_ref[p]
    side_out[0:TQ, :] = hid_ref[...]
    hi, mid, lo = split3(gate_ref[pl.ds(other, 1), :])
    rows = lax.broadcasted_iota(jnp.int32, (8, W), 0)
    packed = jnp.where(rows == 0, hi.astype(F32), jnp.where(rows == 1, mid.astype(F32), lo.astype(F32)))
    side_out[TQ : TQ + 8, :] = packed.astype(BF)


def join_kernel(kv_hbm, got_hbm, out_hbm, sem):
    del kv_hbm
    copy = pltpu.make_async_copy(got_hbm, out_hbm.at[1], sem)
    copy.start()
    copy.wait()


def attend_kernel(xh_id, z0_id, len_ref, q_ref, kv_ref, out_ref):
    scale = HD ** (-0.5) * 1.4426950408889634
    own = xh_id[0]
    at = lax.broadcasted_iota(jnp.int32, (1, NS * TK), 1)
    block = jnp.zeros_like(at)
    for i in range(1, NS):
        block = block + (at >= i * TK).astype(jnp.int32)
    within = at - block * TK
    from_own = (block & 1) == 0
    seq = (jnp.where(from_own, own, 1 - own) * NZ + (block >> 1)) * NZ + z0_id[0]
    dead = (within < TT) & (seq * TT + within >= len_ref[own])
    bias = jnp.where(dead, -1e30, 0.0)
    lane = lax.broadcasted_iota(jnp.int32, (NS * TQ, HD), 1)
    stats = jnp.zeros((NS * TQ, HD), F32)
    for h in range(HPD):
        hs = slice(h * HD, (h + 1) * HD)
        q = q_ref[:, :, hs].reshape(NS * TQ, HD)
        k = kv_ref[:, :, 0, :, hs].reshape(NS * TK, HD)
        v = kv_ref[:, :, 1, :, hs].reshape(NS * TK, HD)
        s = lax.dot_general(q, k, (((1,), (1,)), ((), ())), preferred_element_type=F32)
        s = s * scale + bias
        top = jnp.max(s, -1, keepdims=True)
        e = jnp.exp2(s - top)
        total = jnp.sum(e, -1, keepdims=True)
        o = jnp.dot(e.astype(BF), v, preferred_element_type=F32) / total
        out_ref[:, 0:TQ, hs] = o.astype(BF).reshape(NS, TQ, HD)
        lse = top + jnp.log2(total)
        hi = lse.astype(BF).astype(F32)
        stats = jnp.where(lane == h, hi, jnp.where(lane == HPD + h, lse - hi, stats))
    rows = jnp.transpose(stats)[0:STAT, :].astype(BF)
    for d in range(NS):
        a = (d // 2) * HD
        out_ref[d, TQ : TQ + STAT, 0:HD] = rows[:, a : a + HD]
        out_ref[d, TQ : TQ + STAT, HD:W] = jnp.zeros((STAT, W - HD), BF)


def project_kernel(ids, o_ref, w_ref, out_hbm, attn_ref, out_ref, sems):
    odd = ids[0]
    stats = o_ref[:, TQ : TQ + STAT, 0:HD].astype(F32).reshape(NS * STAT, HD)
    cols = jnp.transpose(jnp.concatenate([stats, stats], 0))
    cols = jnp.where(odd == 0, cols[0:TQ], cols[TQ : 2 * TQ])
    for p in range(2):
        for h in range(HPD):
            hs = slice(h * HD, (h + 1) * HD)
            lses = []
            for z in range(NZ):
                at = (p * NZ + z) * STAT + h
                lses.append(cols[:, at : at + 1] + cols[:, at + HPD : at + HPD + 1])
            top = functools.reduce(jnp.maximum, lses)
            ws = [jnp.exp2(x - top) for x in lses]
            total = functools.reduce(jnp.add, ws)
            acc = jnp.zeros((TQ, HD), F32)
            for z in range(NZ):
                acc = acc + ws[z] * o_ref[p * NZ + z, 0:TQ, hs].astype(F32)
            attn_ref[p * TQ : (p + 1) * TQ, hs] = (acc / total).astype(BF)
    attn = attn_ref[...]
    copies = []
    for b in range(8):
        part = jnp.dot(attn, w_ref[:, b * W : (b + 1) * W], preferred_element_type=F32).astype(BF)
        out_ref[0, b] = part[0:TQ]
        out_ref[1, b] = part[TQ : 2 * TQ]
        copy = pltpu.make_async_copy(out_ref.at[:, b], out_hbm.at[:, b], sems.at[b])
        copy.start()
        copies.append(copy)
    for copy in copies:
        copy.wait()


def finish_kernel(ids, scal, part_ref, hid_ref, gate_ref, side_ref, bias_ref, lat_ref, guided_ref, next_ref):
    mine = ids[0]
    mine_f = mine.astype(F32)
    outs = []
    other_gate = (
        side_ref[TQ : TQ + 1, :].astype(F32) + side_ref[TQ + 1 : TQ + 2, :].astype(F32)
    ) + side_ref[TQ + 2 : TQ + 3, :].astype(F32)
    for g in range(2):
        acc = part_ref[g * 8].astype(F32)
        for b in range(1, 8):
            acc = acc + part_ref[g * 8 + b].astype(F32)
        own = mine == g
        hidden = jnp.where(own, hid_ref[mine].astype(F32), side_ref[0:TQ, :].astype(F32))
        gate = jnp.where(own, gate_ref[pl.ds(mine, 1), :], other_gate)
        outs.append((hidden + gate * (acc + bias_ref[...])).astype(BF).astype(F32))
    cond, uncond = outs
    guided = uncond + scal[0] * (cond - uncond)
    guided_ref[0] = guided.astype(BF)
    next_ref[0] = (lat_ref[0].astype(F32) + scal[1] * guided).astype(BF)


SMEM = functools.partial(pl.BlockSpec, memory_space=pltpu.SMEM)
VMEM = functools.partial(pl.BlockSpec, memory_space=pltpu.VMEM)
HBM = functools.partial(pl.BlockSpec, memory_space=pltpu.HBM)


def call(kernel, outs, ins, out_specs, name, scratch=(), limit=VMEM_LIMIT, cost=None, aliases={}):
    return pl.pallas_call(
        kernel,
        out_shape=outs,
        in_specs=ins,
        out_specs=out_specs,
        scratch_shapes=list(scratch),
        compiler_params=pltpu.CompilerParams(vmem_limit_bytes=limit),
        cost_estimate=cost,
        input_output_aliases=aliases,
        name=name,
    )


def shards(
    img_hidden,
    img_query,
    img_key,
    img_value,
    txt_key,
    txt_value,
    query_gain,
    key_gain,
    gate,
    proj_weight,
    proj_bias,
    guidance,
    text_len,
    step_index,
    latent,
):
    guide = lax.axis_index("g")
    xh = lax.axis_index("xh")
    z1 = lax.axis_index("z1")
    z0 = lax.axis_index("z0")
    seq = (xh * NZ + z1) * NZ + z0
    rows, cols = rope_tables()
    keep, send, q, side = call(
        prepare_kernel,
        (
            jax.ShapeDtypeStruct((2, 2, TK, W), BF),
            jax.ShapeDtypeStruct((2, TK, W), BF),
            jax.ShapeDtypeStruct((NS, TQ, W), BF),
            jax.ShapeDtypeStruct((TQ + 8, W), BF),
        ),
        [SMEM()] * 3 + [HBM()] * 11,
        (VMEM(),) * 4,
        "prepare",
        [
            pltpu.VMEM((2, TQ, W), BF),
            pltpu.VMEM((2, TQ, W), BF),
            pltpu.VMEM((2, TQ, W), BF),
            pltpu.VMEM((2, TT, W), BF),
            pltpu.VMEM((2, TT, W), BF),
            pltpu.VMEM((TQ, W), BF),
            pltpu.VMEM((2, W), F32),
            pltpu.VMEM((1, HD), F32),
            pltpu.VMEM((2, HD), F32),
            pltpu.VMEM((2, 1, HD), F32),
            pltpu.VMEM((2, TQ, HD), F32),
            pltpu.SemaphoreType.DMA((11,)),
        ],
        63 * 1024 * 1024,
    )(
        seq[None],
        xh[None],
        guide[None],
        img_key[0],
        img_query[0],
        img_value[0],
        txt_key[0],
        txt_value[0],
        img_hidden[0],
        gate[0],
        query_gain[None],
        key_gain,
        jnp.asarray(rows),
        jnp.asarray(cols),
    )
    q = lax.all_to_all(q, ("xh", "z0"), 0, 0, tiled=True)
    swap = [(0, 1), (1, 0)]
    got = lax.ppermute(send, "xh", swap)
    kv = call(
        join_kernel,
        pltpu.HBM((2, 2, TK, W), BF),
        [HBM()] * 2,
        HBM(),
        "join",
        [pltpu.SemaphoreType.DMA],
        cost=pl.CostEstimate(flops=10**11, bytes_accessed=10**6, transcendentals=0),
        aliases={0: 0},
    )(keep, got)
    kv = lax.all_gather(kv, "z1", axis=0)

    out = call(
        attend_kernel,
        pltpu.HBM((NS, TQ + STAT, W), BF),
        [SMEM()] * 3 + [VMEM()] * 2,
        VMEM(),
        "attend",
    )(xh[None], z0[None], text_len, q, kv)
    out = lax.all_to_all(out, ("xh", "z0"), 0, 0, tiled=True)
    part = call(
        project_kernel,
        jax.ShapeDtypeStruct((2, 8, TQ, W), BF),
        [SMEM()] + [VMEM()] * 2,
        HBM(),
        "project",
        [pltpu.VMEM((2 * TQ, W), BF), pltpu.VMEM((2, 8, TQ, W), BF), pltpu.SemaphoreType.DMA((8,))],
    )((z0 & 1)[None], out, proj_weight)
    side = lax.ppermute(side, "g", swap)
    part = lax.all_to_all(part.reshape(16, TQ, W), ("g", "y", "c"), 0, 0, tiled=True)
    index = step_index[0]
    u_now = 1.0 - index.astype(F32) / STEPS
    u_next = 1.0 - (index + 1).astype(F32) / STEPS
    step = 3.0 * u_next / (1.0 + 2.0 * u_next) - 3.0 * u_now / (1.0 + 2.0 * u_now)
    shape = jax.ShapeDtypeStruct((1, TQ, W), BF)
    return call(finish_kernel, (shape, shape), [SMEM()] * 2 + [VMEM()] * 6, (VMEM(),) * 2, "finish")(
        guide[None],
        jnp.stack([guidance[guide], step]),
        part,
        img_hidden[0],
        gate[0],
        side,
        proj_bias[None],
        latent,
    )


def solution(mesh):
    fine = Mesh(mesh.devices.reshape(2, 2, NZ, NZ, 4, 2), ("g", "xh", "z1", "z0", "y", "c"))
    seq = ("xh", "z1", "z0")
    blk = ("y", "c")
    act = P("g", None, seq, blk)
    return jax.shard_map(
        shards,
        mesh=fine,
        in_specs=(
            act,
            act,
            act,
            act,
            act,
            act,
            P(),
            P(),
            P("g", None, blk),
            P(blk, None),
            P(blk),
            P(),
            P(),
            P(),
            P("g", seq, blk),
        ),
        out_specs=(P("g", seq, blk), P("g", seq, blk)),
        check_vma=False,
    )
```

```python
import functools

import jax
import jax.numpy as jnp
import numpy as np
from jax import lax
from jax.experimental import pallas as pl
from jax.experimental.pallas import tpu as pltpu
from jax.sharding import Mesh, PartitionSpec as P

HD = 128
GRID = 64
STEPS = 8
HPD = 3
W = HPD * HD
TQ = 64
TT = 16
TK = TQ + TT
NZ = 4
NS = 8
STAT = 8
BF = jnp.bfloat16
F32 = jnp.float32
VMEM_LIMIT = 48 * 1024 * 1024


def rope_tables():
    first = HD // 8
    second = (HD - first) // 2
    freqs = 10000.0 ** (-np.arange(0, second, 2).astype(np.float64) / second)
    n = freqs.shape[0]
    lane = np.arange(HD)
    pair = lane // 2
    sign = np.where(lane % 2 == 0, -1.0, 1.0)
    row_f = np.where((pair >= first // 2) & (pair < first // 2 + n), freqs[np.clip(pair - first // 2, 0, n - 1)], 0.0)
    col_f = np.where(pair >= first // 2 + n, freqs[np.clip(pair - first // 2 - n, 0, n - 1)], 0.0)
    rows = np.arange(32)[:, None] * row_f[None]
    cols = np.arange(GRID)[:, None] * col_f[None]
    return (
        np.stack([np.cos(rows), np.sin(rows) * sign]).astype(np.float32),
        np.stack([np.cos(cols), np.sin(cols) * sign]).astype(np.float32),
    )


def split3(x):
    hi = x.astype(BF)
    rest = x - hi.astype(F32)
    mid = rest.astype(BF)
    lo = (rest - mid.astype(F32)).astype(BF)
    return hi, mid, lo


def rope_of(row_ref, col_ref):
    in_row = lax.broadcasted_iota(jnp.int32, (TQ, HD), 1) < 72
    return jnp.where(in_row, row_ref[0], col_ref[0]), jnp.where(in_row, row_ref[1], col_ref[1])


def normed(x, gain):
    x = x.astype(F32)
    return x * lax.rsqrt(jnp.mean(x * x, -1, keepdims=True) + 1e-06) * gain


def rotated(x, table):
    even = lax.broadcasted_iota(jnp.int32, (TQ, HD), 1) % 2 == 0
    swapped = jnp.where(even, pltpu.roll(x, HD - 1, 1), pltpu.roll(x, 1, 1))
    return x * table[0] + swapped * table[1]


def start_all(pairs, sems):
    copies = [pltpu.make_async_copy(src, dst, sems.at[i]) for i, (src, dst) in enumerate(pairs)]
    for copy in copies:
        copy.start()
    return copies


def prepare_kernel(
    seq_id, xh_id, guide_id, k_hbm, q_hbm, v_hbm, tk_hbm, tv_hbm, hid_hbm, gate_hbm, qg_hbm, kg_hbm, row_hbm, col_hbm,
    keep_out, send_out, q_out, side_out,
    k_ref, q_ref, v_ref, tk_ref, tv_ref, hid_ref, gate_ref, qg_ref, kg_ref, row_ref, col_ref, sems,
):
    other = 1 - guide_id[0]
    rows = row_hbm.at[:, pl.ds(seq_id[0], 1)]
    copies = start_all(
        (
            (rows, row_ref), (col_hbm, col_ref), (qg_hbm, qg_ref), (q_hbm, q_ref), (kg_hbm, kg_ref), (tk_hbm, tk_ref), (k_hbm, k_ref),
            (v_hbm, v_ref), (tv_hbm, tv_ref), (hid_hbm.at[other], hid_ref), (gate_hbm, gate_ref),
        ),
        sems,
    )
    for copy in copies[:4]:
        copy.wait()
    table = rope_of(row_ref, col_ref)
    for p in range(2):
        for h in range(HPD):
            hs = slice(h * HD, (h + 1) * HD)
            q = rotated(normed(q_ref[p, :, hs], qg_ref[...]), table).astype(BF)
            for z in range(NZ):
                q_out[p * NZ + z, :, hs] = q
    for copy in copies[4:7]:
        copy.wait()
    own = xh_id[0]
    for out, p in ((keep_out.at[0], own), (send_out, 1 - own)):
        for h in range(HPD):
            hs = slice(h * HD, (h + 1) * HD)
            out[0, 0:TT, hs] = normed(tk_ref[p, :, hs], kg_ref[1:2]).astype(BF)
            out[0, TT:TK, hs] = rotated(normed(k_ref[p, :, hs], kg_ref[0:1]), table).astype(BF)
    for copy in copies[7:]:
        copy.wait()
    for out, p in ((keep_out.at[0], own), (send_out, 1 - own)):
        out[1, 0:TT, :] = tv_ref[p]
        out[1, TT:TK, :] = v_ref[p]
    side_out[0:TQ, :] = hid_ref[...]
    hi, mid, lo = split3(gate_ref[pl.ds(other, 1), :])
    rows = lax.broadcasted_iota(jnp.int32, (8, W), 0)
    packed = jnp.where(rows == 0, hi.astype(F32), jnp.where(rows == 1, mid.astype(F32), lo.astype(F32)))
    side_out[TQ : TQ + 8, :] = packed.astype(BF)


def join_kernel(kv_hbm, got_hbm, out_hbm, sem):
    del kv_hbm
    copy = pltpu.make_async_copy(got_hbm, out_hbm.at[1], sem)
    copy.start()
    copy.wait()


def attend_kernel(xh_id, z0_id, len_ref, q_ref, kv_ref, out_ref):
    scale = HD ** (-0.5) * 1.4426950408889634
    own = xh_id[0]
    at = lax.broadcasted_iota(jnp.int32, (1, NS * TK), 1)
    block = jnp.zeros_like(at)
    for i in range(1, NS):
        block = block + (at >= i * TK).astype(jnp.int32)
    within = at - block * TK
    from_own = (block & 1) == 0
    seq = (jnp.where(from_own, own, 1 - own) * NZ + (block >> 1)) * NZ + z0_id[0]
    dead = (within < TT) & (seq * TT + within >= len_ref[own])
    bias = jnp.where(dead, -1e30, 0.0)
    lane = lax.broadcasted_iota(jnp.int32, (NS * TQ, HD), 1)
    stats = jnp.zeros((NS * TQ, HD), F32)
    for h in range(HPD):
        hs = slice(h * HD, (h + 1) * HD)
        q = q_ref[:, :, hs].reshape(NS * TQ, HD)
        k = kv_ref[:, :, 0, :, hs].reshape(NS * TK, HD)
        v = kv_ref[:, :, 1, :, hs].reshape(NS * TK, HD)
        s = lax.dot_general(q, k, (((1,), (1,)), ((), ())), preferred_element_type=F32)
        s = s * scale + bias
        top = jnp.max(s, -1, keepdims=True)
        e = jnp.exp2(s - top)
        total = jnp.sum(e, -1, keepdims=True)
        o = jnp.dot(e.astype(BF), v, preferred_element_type=F32) / total
        out_ref[:, 0:TQ, hs] = o.astype(BF).reshape(NS, TQ, HD)
        lse = top + jnp.log2(total)
        hi = lse.astype(BF).astype(F32)
        stats = jnp.where(lane == h, hi, jnp.where(lane == HPD + h, lse - hi, stats))
    rows = jnp.transpose(stats)[0:STAT, :].astype(BF)
    for d in range(NS):
        a = (d // 2) * HD
        out_ref[d, TQ : TQ + STAT, 0:HD] = rows[:, a : a + HD]
        out_ref[d, TQ : TQ + STAT, HD:W] = jnp.zeros((STAT, W - HD), BF)


def project_kernel(ids, o_ref, w_ref, out_hbm, attn_ref, out_ref, sems):
    odd = ids[0]
    stats = o_ref[:, TQ : TQ + STAT, 0:HD].astype(F32).reshape(NS * STAT, HD)
    cols = jnp.transpose(jnp.concatenate([stats, stats], 0))
    cols = jnp.where(odd == 0, cols[0:TQ], cols[TQ : 2 * TQ])
    for p in range(2):
        for h in range(HPD):
            hs = slice(h * HD, (h + 1) * HD)
            lses = []
            for z in range(NZ):
                at = (p * NZ + z) * STAT + h
                lses.append(cols[:, at : at + 1] + cols[:, at + HPD : at + HPD + 1])
            top = functools.reduce(jnp.maximum, lses)
            ws = [jnp.exp2(x - top) for x in lses]
            total = functools.reduce(jnp.add, ws)
            acc = jnp.zeros((TQ, HD), F32)
            for z in range(NZ):
                acc = acc + ws[z] * o_ref[p * NZ + z, 0:TQ, hs].astype(F32)
            attn_ref[p * TQ : (p + 1) * TQ, hs] = (acc / total).astype(BF)
    attn = attn_ref[...]
    copies = []
    for b in range(8):
        part = jnp.dot(attn, w_ref[:, b * W : (b + 1) * W], preferred_element_type=F32).astype(BF)
        out_ref[0, b] = part[0:TQ]
        out_ref[1, b] = part[TQ : 2 * TQ]
        copy = pltpu.make_async_copy(out_ref.at[:, b], out_hbm.at[:, b], sems.at[b])
        copy.start()
        copies.append(copy)
    for copy in copies:
        copy.wait()


def finish_kernel(ids, scal, part_ref, hid_ref, gate_ref, side_ref, bias_ref, lat_ref, guided_ref, next_ref):
    mine = ids[0]
    mine_f = mine.astype(F32)
    outs = []
    other_gate = (
        side_ref[TQ : TQ + 1, :].astype(F32) + side_ref[TQ + 1 : TQ + 2, :].astype(F32)
    ) + side_ref[TQ + 2 : TQ + 3, :].astype(F32)
    for g in range(2):
        acc = part_ref[g * 8].astype(F32)
        for b in range(1, 8):
            acc = acc + part_ref[g * 8 + b].astype(F32)
        own = mine == g
        hidden = jnp.where(own, hid_ref[mine].astype(F32), side_ref[0:TQ, :].astype(F32))
        gate = jnp.where(own, gate_ref[pl.ds(mine, 1), :], other_gate)
        outs.append((hidden + gate * (acc + bias_ref[...])).astype(BF).astype(F32))
    cond, uncond = outs
    guided = uncond + scal[0] * (cond - uncond)
    guided_ref[0] = guided.astype(BF)
    next_ref[0] = (lat_ref[0].astype(F32) + scal[1] * guided).astype(BF)


SMEM = functools.partial(pl.BlockSpec, memory_space=pltpu.SMEM)
VMEM = functools.partial(pl.BlockSpec, memory_space=pltpu.VMEM)
HBM = functools.partial(pl.BlockSpec, memory_space=pltpu.HBM)


def call(kernel, outs, ins, out_specs, name, scratch=(), limit=VMEM_LIMIT, cost=None, aliases={}):
    return pl.pallas_call(
        kernel,
        out_shape=outs,
        in_specs=ins,
        out_specs=out_specs,
        scratch_shapes=list(scratch),
        compiler_params=pltpu.CompilerParams(vmem_limit_bytes=limit),
        cost_estimate=cost,
        input_output_aliases=aliases,
        name=name,
    )


def exchange(x):
    groups = []
    for core in range(2):
        for first in range(2 * core, 16 + 2 * core, NZ):
            groups.append([(half * 16 + (first + i) % 16) * 2 + core for half in range(2) for i in range(NZ)])
    return lax.all_to_all(x, ("xh", "z1", "z0", "c"), 0, 0, tiled=True, axis_index_groups=groups)


def shards(
    img_hidden,
    img_query,
    img_key,
    img_value,
    txt_key,
    txt_value,
    query_gain,
    key_gain,
    gate,
    proj_weight,
    proj_bias,
    guidance,
    text_len,
    step_index,
    latent,
):
    guide = lax.axis_index("g")
    xh = lax.axis_index("xh")
    z1 = lax.axis_index("z1")
    z0 = lax.axis_index("z0")
    seq = (xh * NZ + z1) * NZ + z0
    rows, cols = rope_tables()
    keep, send, q, side = call(
        prepare_kernel,
        (
            jax.ShapeDtypeStruct((2, 2, TK, W), BF),
            jax.ShapeDtypeStruct((2, TK, W), BF),
            jax.ShapeDtypeStruct((NS, TQ, W), BF),
            jax.ShapeDtypeStruct((TQ + 8, W), BF),
        ),
        [SMEM()] * 3 + [HBM()] * 11,
        (VMEM(),) * 4,
        "prepare",
        [
            pltpu.VMEM((2, TQ, W), BF),
            pltpu.VMEM((2, TQ, W), BF),
            pltpu.VMEM((2, TQ, W), BF),
            pltpu.VMEM((2, TT, W), BF),
            pltpu.VMEM((2, TT, W), BF),
            pltpu.VMEM((TQ, W), BF),
            pltpu.VMEM((2, W), F32),
            pltpu.VMEM((1, HD), F32),
            pltpu.VMEM((2, HD), F32),
            pltpu.VMEM((2, 1, HD), F32),
            pltpu.VMEM((2, TQ, HD), F32),
            pltpu.SemaphoreType.DMA((11,)),
        ],
        63 * 1024 * 1024,
    )(
        seq[None],
        xh[None],
        guide[None],
        img_key[0],
        img_query[0],
        img_value[0],
        txt_key[0],
        txt_value[0],
        img_hidden[0],
        gate[0],
        query_gain[None],
        key_gain,
        jnp.asarray(rows),
        jnp.asarray(cols),
    )
    q = exchange(q)
    swap = [(0, 1), (1, 0)]
    got = lax.ppermute(send, "xh", swap)
    kv = call(
        join_kernel,
        pltpu.HBM((2, 2, TK, W), BF),
        [HBM()] * 2,
        HBM(),
        "join",
        [pltpu.SemaphoreType.DMA],
        cost=pl.CostEstimate(flops=10**11, bytes_accessed=10**6, transcendentals=0),
        aliases={0: 0},
    )(keep, got)
    kv = lax.all_gather(kv, "z1", axis=0)

    out = call(
        attend_kernel,
        pltpu.HBM((NS, TQ + STAT, W), BF),
        [SMEM()] * 3 + [VMEM()] * 2,
        VMEM(),
        "attend",
    )(xh[None], z0[None], text_len, q, kv)
    out = exchange(out)
    part = call(
        project_kernel,
        jax.ShapeDtypeStruct((2, 8, TQ, W), BF),
        [SMEM()] + [VMEM()] * 2,
        HBM(),
        "project",
        [pltpu.VMEM((2 * TQ, W), BF), pltpu.VMEM((2, 8, TQ, W), BF), pltpu.SemaphoreType.DMA((8,))],
    )((z0 & 1)[None], out, proj_weight)
    side = lax.ppermute(side, "g", swap)
    part = lax.all_to_all(part.reshape(16, TQ, W), ("g", "y", "c"), 0, 0, tiled=True)
    index = step_index[0]
    u_now = 1.0 - index.astype(F32) / STEPS
    u_next = 1.0 - (index + 1).astype(F32) / STEPS
    step = 3.0 * u_next / (1.0 + 2.0 * u_next) - 3.0 * u_now / (1.0 + 2.0 * u_now)
    shape = jax.ShapeDtypeStruct((1, TQ, W), BF)
    return call(finish_kernel, (shape, shape), [SMEM()] * 2 + [VMEM()] * 6, (VMEM(),) * 2, "finish")(
        guide[None],
        jnp.stack([guidance[guide], step]),
        part,
        img_hidden[0],
        gate[0],
        side,
        proj_bias[None],
        latent,
    )


def solution(mesh):
    fine = Mesh(mesh.devices.reshape(2, 2, NZ, NZ, 4, 2), ("g", "xh", "z1", "z0", "y", "c"))
    seq = ("xh", "z1", "z0")
    blk = ("y", "c")
    act = P("g", None, seq, blk)
    return jax.shard_map(
        shards,
        mesh=fine,
        in_specs=(
            act,
            act,
            act,
            act,
            act,
            act,
            P(),
            P(),
            P("g", None, blk),
            P(blk, None),
            P(blk),
            P(),
            P(),
            P(),
            P("g", seq, blk),
        ),
        out_specs=(P("g", seq, blk), P("g", seq, blk)),
        check_vma=False,
    )
```

```python
import functools

import jax
import jax.numpy as jnp
import numpy as np
from jax import lax
from jax.experimental import pallas as pl
from jax.experimental.pallas import tpu as pltpu
from jax.sharding import Mesh, PartitionSpec as P

HD = 128
GRID = 64
STEPS = 8
HPD = 3
W = HPD * HD
TQ = 64
TT = 16
TK = TQ + TT
NZ = 4
NS = 8
STAT = 8
BF = jnp.bfloat16
F32 = jnp.float32
VMEM_LIMIT = 48 * 1024 * 1024


def rope_tables():
    first = HD // 8
    second = (HD - first) // 2
    freqs = 10000.0 ** (-np.arange(0, second, 2).astype(np.float64) / second)
    n = freqs.shape[0]
    lane = np.arange(HD)
    pair = lane // 2
    sign = np.where(lane % 2 == 0, -1.0, 1.0)
    row_f = np.where((pair >= first // 2) & (pair < first // 2 + n), freqs[np.clip(pair - first // 2, 0, n - 1)], 0.0)
    col_f = np.where(pair >= first // 2 + n, freqs[np.clip(pair - first // 2 - n, 0, n - 1)], 0.0)
    rows = np.arange(32)[:, None] * row_f[None]
    cols = np.arange(GRID)[:, None] * col_f[None]
    return (
        np.stack([np.cos(rows), np.sin(rows) * sign]).astype(np.float32),
        np.stack([np.cos(cols), np.sin(cols) * sign]).astype(np.float32),
    )


def split3(x):
    hi = x.astype(BF)
    rest = x - hi.astype(F32)
    mid = rest.astype(BF)
    lo = (rest - mid.astype(F32)).astype(BF)
    return hi, mid, lo


def rope_of(row_ref, col_ref):
    in_row = lax.broadcasted_iota(jnp.int32, (TQ, HD), 1) < 72
    return jnp.where(in_row, row_ref[0], col_ref[0]), jnp.where(in_row, row_ref[1], col_ref[1])


def normed(x, gain):
    x = x.astype(F32)
    return x * lax.rsqrt(jnp.mean(x * x, -1, keepdims=True) + 1e-06) * gain


def rotated(x, table):
    even = lax.broadcasted_iota(jnp.int32, (TQ, HD), 1) % 2 == 0
    swapped = jnp.where(even, pltpu.roll(x, HD - 1, 1), pltpu.roll(x, 1, 1))
    return x * table[0] + swapped * table[1]


def start_all(pairs, sems):
    copies = [pltpu.make_async_copy(src, dst, sems.at[i]) for i, (src, dst) in enumerate(pairs)]
    for copy in copies:
        copy.start()
    return copies


def prepare_kernel(
    seq_id, xh_id, guide_id, k_hbm, q_hbm, v_hbm, tk_hbm, tv_hbm, hid_hbm, gate_hbm, qg_hbm, kg_hbm, row_hbm, col_hbm,
    keep_out, send_out, q_hbm_out, side_out,
    k_ref, q_ref, v_ref, tk_ref, tv_ref, hid_ref, gate_ref, qg_ref, kg_ref, row_ref, col_ref, q_out, sems, q_sems,
):
    other = 1 - guide_id[0]
    rows = row_hbm.at[:, pl.ds(seq_id[0], 1)]
    copies = start_all(
        (
            (rows, row_ref), (col_hbm, col_ref), (qg_hbm, qg_ref), (q_hbm, q_ref), (kg_hbm, kg_ref), (tk_hbm, tk_ref), (k_hbm, k_ref),
            (v_hbm, v_ref), (tv_hbm, tv_ref), (hid_hbm.at[other], hid_ref), (gate_hbm, gate_ref),
        ),
        sems,
    )
    for copy in copies[:4]:
        copy.wait()
    table = rope_of(row_ref, col_ref)
    sent = []
    for p in range(2):
        for h in range(HPD):
            hs = slice(h * HD, (h + 1) * HD)
            q_out[p, :, hs] = rotated(normed(q_ref[p, :, hs], qg_ref[...]), table).astype(BF)
        slots = [p * NZ + z for z in range(NZ)]
        sent += start_all([(q_out.at[p], q_hbm_out.at[d]) for d in slots], q_sems.at[pl.ds(p * NZ, NZ)])
    for copy in copies[4:7]:
        copy.wait()
    own = xh_id[0]
    for out, p in ((keep_out.at[0], own), (send_out, 1 - own)):
        for h in range(HPD):
            hs = slice(h * HD, (h + 1) * HD)
            out[0, 0:TT, hs] = normed(tk_ref[p, :, hs], kg_ref[1:2]).astype(BF)
            out[0, TT:TK, hs] = rotated(normed(k_ref[p, :, hs], kg_ref[0:1]), table).astype(BF)
    for copy in copies[7:]:
        copy.wait()
    for out, p in ((keep_out.at[0], own), (send_out, 1 - own)):
        out[1, 0:TT, :] = tv_ref[p]
        out[1, TT:TK, :] = v_ref[p]
    side_out[0:TQ, :] = hid_ref[...]
    hi, mid, lo = split3(gate_ref[pl.ds(other, 1), :])
    rows = lax.broadcasted_iota(jnp.int32, (8, W), 0)
    packed = jnp.where(rows == 0, hi.astype(F32), jnp.where(rows == 1, mid.astype(F32), lo.astype(F32)))
    side_out[TQ : TQ + 8, :] = packed.astype(BF)
    for copy in sent:
        copy.wait()


def join_kernel(kv_hbm, got_hbm, out_hbm, sem):
    del kv_hbm
    copy = pltpu.make_async_copy(got_hbm, out_hbm.at[1], sem)
    copy.start()
    copy.wait()


def attend_kernel(xh_id, z0_id, len_ref, q_ref, kv_ref, out_ref):
    scale = HD ** (-0.5) * 1.4426950408889634
    own = xh_id[0]
    at = lax.broadcasted_iota(jnp.int32, (1, NS * TK), 1)
    block = jnp.zeros_like(at)
    for i in range(1, NS):
        block = block + (at >= i * TK).astype(jnp.int32)
    within = at - block * TK
    from_own = (block & 1) == 0
    seq = (jnp.where(from_own, own, 1 - own) * NZ + (block >> 1)) * NZ + z0_id[0]
    dead = (within < TT) & (seq * TT + within >= len_ref[own])
    bias = jnp.where(dead, -1e30, 0.0)
    lane = lax.broadcasted_iota(jnp.int32, (NS * TQ, HD), 1)
    stats = jnp.zeros((NS * TQ, HD), F32)
    for h in range(HPD):
        hs = slice(h * HD, (h + 1) * HD)
        q = q_ref[:, :, hs].reshape(NS * TQ, HD)
        k = kv_ref[:, :, 0, :, hs].reshape(NS * TK, HD)
        v = kv_ref[:, :, 1, :, hs].reshape(NS * TK, HD)
        s = lax.dot_general(q, k, (((1,), (1,)), ((), ())), preferred_element_type=F32)
        s = s * scale + bias
        top = jnp.max(s, -1, keepdims=True)
        e = jnp.exp2(s - top)
        total = jnp.sum(e, -1, keepdims=True)
        o = jnp.dot(e.astype(BF), v, preferred_element_type=F32) / total
        out_ref[:, 0:TQ, hs] = o.astype(BF).reshape(NS, TQ, HD)
        lse = top + jnp.log2(total)
        hi = lse.astype(BF).astype(F32)
        stats = jnp.where(lane == h, hi, jnp.where(lane == HPD + h, lse - hi, stats))
    rows = jnp.transpose(stats)[0:STAT, :].astype(BF)
    for d in range(NS):
        a = (d // 2) * HD
        out_ref[d, TQ : TQ + STAT, 0:HD] = rows[:, a : a + HD]
        out_ref[d, TQ : TQ + STAT, HD:W] = jnp.zeros((STAT, W - HD), BF)


def project_kernel(ids, o_ref, w_ref, out_hbm, attn_ref, out_ref, sems):
    odd = ids[0]
    stats = o_ref[:, TQ : TQ + STAT, 0:HD].astype(F32).reshape(NS * STAT, HD)
    cols = jnp.transpose(jnp.concatenate([stats, stats], 0))
    cols = jnp.where(odd == 0, cols[0:TQ], cols[TQ : 2 * TQ])
    for p in range(2):
        for h in range(HPD):
            hs = slice(h * HD, (h + 1) * HD)
            lses = []
            for z in range(NZ):
                at = (p * NZ + z) * STAT + h
                lses.append(cols[:, at : at + 1] + cols[:, at + HPD : at + HPD + 1])
            top = functools.reduce(jnp.maximum, lses)
            ws = [jnp.exp2(x - top) for x in lses]
            total = functools.reduce(jnp.add, ws)
            acc = jnp.zeros((TQ, HD), F32)
            for z in range(NZ):
                acc = acc + ws[z] * o_ref[p * NZ + z, 0:TQ, hs].astype(F32)
            attn_ref[p * TQ : (p + 1) * TQ, hs] = (acc / total).astype(BF)
    attn = attn_ref[...]
    copies = []
    for b in range(8):
        part = jnp.dot(attn, w_ref[:, b * W : (b + 1) * W], preferred_element_type=F32).astype(BF)
        out_ref[0, b] = part[0:TQ]
        out_ref[1, b] = part[TQ : 2 * TQ]
        copy = pltpu.make_async_copy(out_ref.at[:, b], out_hbm.at[:, b], sems.at[b])
        copy.start()
        copies.append(copy)
    for copy in copies:
        copy.wait()


def finish_kernel(ids, scal, part_ref, hid_ref, gate_ref, side_ref, bias_ref, lat_ref, guided_ref, next_ref):
    mine = ids[0]
    mine_f = mine.astype(F32)
    outs = []
    other_gate = (
        side_ref[TQ : TQ + 1, :].astype(F32) + side_ref[TQ + 1 : TQ + 2, :].astype(F32)
    ) + side_ref[TQ + 2 : TQ + 3, :].astype(F32)
    for g in range(2):
        acc = part_ref[g * 8].astype(F32)
        for b in range(1, 8):
            acc = acc + part_ref[g * 8 + b].astype(F32)
        own = mine == g
        hidden = jnp.where(own, hid_ref[mine].astype(F32), side_ref[0:TQ, :].astype(F32))
        gate = jnp.where(own, gate_ref[pl.ds(mine, 1), :], other_gate)
        outs.append((hidden + gate * (acc + bias_ref[...])).astype(BF).astype(F32))
    cond, uncond = outs
    guided = uncond + scal[0] * (cond - uncond)
    guided_ref[0] = guided.astype(BF)
    next_ref[0] = (lat_ref[0].astype(F32) + scal[1] * guided).astype(BF)


SMEM = functools.partial(pl.BlockSpec, memory_space=pltpu.SMEM)
VMEM = functools.partial(pl.BlockSpec, memory_space=pltpu.VMEM)
HBM = functools.partial(pl.BlockSpec, memory_space=pltpu.HBM)


def call(kernel, outs, ins, out_specs, name, scratch=(), limit=VMEM_LIMIT, cost=None, aliases={}):
    return pl.pallas_call(
        kernel,
        out_shape=outs,
        in_specs=ins,
        out_specs=out_specs,
        scratch_shapes=list(scratch),
        compiler_params=pltpu.CompilerParams(vmem_limit_bytes=limit),
        cost_estimate=cost,
        input_output_aliases=aliases,
        name=name,
    )


def exchange(x):
    groups = []
    for core in range(2):
        for first in range(2 * core, 16 + 2 * core, NZ):
            groups.append([(half * 16 + (first + i) % 16) * 2 + core for half in range(2) for i in range(NZ)])
    return lax.all_to_all(x, ("xh", "z1", "z0", "c"), 0, 0, tiled=True, axis_index_groups=groups)


def shards(
    img_hidden,
    img_query,
    img_key,
    img_value,
    txt_key,
    txt_value,
    query_gain,
    key_gain,
    gate,
    proj_weight,
    proj_bias,
    guidance,
    text_len,
    step_index,
    latent,
):
    guide = lax.axis_index("g")
    xh = lax.axis_index("xh")
    z1 = lax.axis_index("z1")
    z0 = lax.axis_index("z0")
    seq = (xh * NZ + z1) * NZ + z0
    rows, cols = rope_tables()
    keep, send, q, side = call(
        prepare_kernel,
        (
            jax.ShapeDtypeStruct((2, 2, TK, W), BF),
            jax.ShapeDtypeStruct((2, TK, W), BF),
            jax.ShapeDtypeStruct((NS, TQ, W), BF),
            jax.ShapeDtypeStruct((TQ + 8, W), BF),
        ),
        [SMEM()] * 3 + [HBM()] * 11,
        (VMEM(), VMEM(), HBM(), VMEM()),
        "prepare",
        [
            pltpu.VMEM((2, TQ, W), BF),
            pltpu.VMEM((2, TQ, W), BF),
            pltpu.VMEM((2, TQ, W), BF),
            pltpu.VMEM((2, TT, W), BF),
            pltpu.VMEM((2, TT, W), BF),
            pltpu.VMEM((TQ, W), BF),
            pltpu.VMEM((2, W), F32),
            pltpu.VMEM((1, HD), F32),
            pltpu.VMEM((2, HD), F32),
            pltpu.VMEM((2, 1, HD), F32),
            pltpu.VMEM((2, TQ, HD), F32),
            pltpu.VMEM((2, TQ, W), BF),
            pltpu.SemaphoreType.DMA((11,)),
            pltpu.SemaphoreType.DMA((NS,)),
        ],
        63 * 1024 * 1024,
    )(
        seq[None],
        xh[None],
        guide[None],
        img_key[0],
        img_query[0],
        img_value[0],
        txt_key[0],
        txt_value[0],
        img_hidden[0],
        gate[0],
        query_gain[None],
        key_gain,
        jnp.asarray(rows),
        jnp.asarray(cols),
    )
    q = exchange(q)
    swap = [(0, 1), (1, 0)]
    got = lax.ppermute(send, "xh", swap)
    kv = call(
        join_kernel,
        pltpu.HBM((2, 2, TK, W), BF),
        [HBM()] * 2,
        HBM(),
        "join",
        [pltpu.SemaphoreType.DMA],
        cost=pl.CostEstimate(flops=10**11, bytes_accessed=10**6, transcendentals=0),
        aliases={0: 0},
    )(keep, got)
    kv = lax.all_gather(kv, "z1", axis=0)

    out = call(
        attend_kernel,
        pltpu.HBM((NS, TQ + STAT, W), BF),
        [SMEM()] * 3 + [VMEM()] * 2,
        VMEM(),
        "attend",
    )(xh[None], z0[None], text_len, q, kv)
    out = exchange(out)
    part = call(
        project_kernel,
        jax.ShapeDtypeStruct((2, 8, TQ, W), BF),
        [SMEM()] + [VMEM()] * 2,
        HBM(),
        "project",
        [pltpu.VMEM((2 * TQ, W), BF), pltpu.VMEM((2, 8, TQ, W), BF), pltpu.SemaphoreType.DMA((8,))],
    )((z0 & 1)[None], out, proj_weight)
    side = lax.ppermute(side, "g", swap)
    part = lax.all_to_all(part.reshape(16, TQ, W), ("g", "y", "c"), 0, 0, tiled=True)
    index = step_index[0]
    u_now = 1.0 - index.astype(F32) / STEPS
    u_next = 1.0 - (index + 1).astype(F32) / STEPS
    step = 3.0 * u_next / (1.0 + 2.0 * u_next) - 3.0 * u_now / (1.0 + 2.0 * u_now)
    shape = jax.ShapeDtypeStruct((1, TQ, W), BF)
    return call(finish_kernel, (shape, shape), [SMEM()] * 2 + [VMEM()] * 6, (VMEM(),) * 2, "finish")(
        guide[None],
        jnp.stack([guidance[guide], step]),
        part,
        img_hidden[0],
        gate[0],
        side,
        proj_bias[None],
        latent,
    )


def solution(mesh):
    fine = Mesh(mesh.devices.reshape(2, 2, NZ, NZ, 4, 2), ("g", "xh", "z1", "z0", "y", "c"))
    seq = ("xh", "z1", "z0")
    blk = ("y", "c")
    act = P("g", None, seq, blk)
    return jax.shard_map(
        shards,
        mesh=fine,
        in_specs=(
            act,
            act,
            act,
            act,
            act,
            act,
            P(),
            P(),
            P("g", None, blk),
            P(blk, None),
            P(blk),
            P(),
            P(),
            P(),
            P("g", seq, blk),
        ),
        out_specs=(P("g", seq, blk), P("g", seq, blk)),
        check_vma=False,
    )
```
